256 devices in a mesh: win: 4 (over y_lo, core), tile: 64 (over x, y_hi, z).
Axes of the slice: x: 4, y: 4 (y_hi: 2, y_lo: 2; y = y_hi * 2 + y_lo), z: 8, core: 2. Of those that a mesh axis runs over, the one named last changes fastest.
Arguments:
- initial: float32 [4, 64, 36, 4096], P('win', 'tile'), may hold values from -6 to 6
- courant_x: bfloat16 [4, 64, 36, 4096], P('win', 'tile'), may hold values from 0.099609375 to 2.890625
- courant_y: bfloat16 [4, 64, 36, 4096], P('win', 'tile'), may hold values from 0.099609375 to 2.890625
- observed: float32 [4, 64, 64, 64], P('win', 'tile'), may hold values from -3 to 3
- precision_w: float32 [4, 64, 64, 64], P('win', 'tile'), may hold values from 0.2 to 2
- kernel: float32 [36], replicated, may hold values from 0.1 to 1
- profile: float32 [36], replicated, may hold values from 0.05 to 1
- emission: float32 [64, 64, 64], P('tile'), may hold values from -6 to 6
- edges: int32 [6, 64], replicated, may hold values from 0 to 63, as said below
Outputs:
- gradient: float32 [64, 64, 64], P('tile', 'win')
The draws below stay inside these ranges and needn't reach their ends.
Inputs may be any that keep to these rules, and one draw needn't show every extreme that they name: edges[0, t] is (t - 1) or (t - 16) modulo 64, and edges[3, t] is (t - 2) or (t - 32) modulo 64; each of the four occurs for some tile; rows 1, 2, 4 and 5 hold 0 or 1, each value at some tile.
All inputs are finite; a program needn't handle non-finite values.
Results may differ from the reference program's by a relative error of at most 0.0003.
Values sent between devices are 32-bit elements; how exact they have to be, the bound alone decides.
A program may use at most 64 MiB of HBM per device.

```python
import math
import jax
import jax.numpy as jnp
from jax import lax

SIDE = 64
LEV = 36
STEPS = 2
WINDOWS = 4
TILES = 64


def forced_bits(key):
    bits = jax.random.randint(key, (TILES,), 0, 2)
    order = jax.random.permutation(jax.random.fold_in(key, 7), TILES)
    return bits.at[order[0]].set(0).at[order[1]].set(1)


def draw_edges(key, part):
    positions = jnp.arange(TILES)
    rows = []
    for number, pair in enumerate([(1, TILES // 4), (2, TILES // 2)]):
        branch_key = jax.random.fold_in(key, 11 + number)
        pick = forced_bits(jax.random.fold_in(branch_key, 1))
        offset = jnp.where(pick == 0, pair[0], pair[1])
        rows.append((positions - offset) % TILES)
        rows.append(forced_bits(jax.random.fold_in(branch_key, 2)))
        rows.append(forced_bits(jax.random.fold_in(branch_key, 3)))
    return jnp.stack(rows).astype(jnp.int32)


def shard_levels(key, shape, cuts, low, largest):
    def one(axis_at, shards_of):
        heights = jax.random.uniform(jax.random.fold_in(jax.random.fold_in(key, 6), axis_at), (shards_of,), jnp.float32, low / len(cuts), largest / len(cuts))
        return jnp.repeat(jnp.exp(heights), shape[axis_at] // shards_of).reshape((-1,) + (1,) * (len(shape) - axis_at - 1))

    gain = one(*cuts[0])
    for cut in cuts[1:]:
        gain = gain * one(*cut)
    return gain


def bell_draw(key, dims, spread, bound, shards=(), kind=jnp.bfloat16):
    values = jax.random.normal(key, dims, jnp.float32) * spread
    if len(shards) > 0:
        values = shard_levels(key, dims, shards, -0.22, 0.18) * values
    return jnp.clip(values, min=-bound, max=bound).astype(kind)


def setup_inputs(seed: int = 0) -> dict:
    streams_of = jax.random.split(jax.random.key(seed), 10)
    return {
        "initial": bell_draw(streams_of[0], (WINDOWS, TILES, LEV, SIDE * SIDE), 1.0, 6.0, ((0, 4), (1, 64)), jnp.float32),
        "courant_x": jnp.clip(0.099609375 + 2.7910156 * jax.random.uniform(streams_of[1], (WINDOWS, TILES, LEV, SIDE * SIDE), jnp.float32) ** shard_levels(streams_of[1], (WINDOWS, TILES, LEV, SIDE * SIDE), ((0, 4), (1, 64)), -0.2, 0.2), 0.099609375, 2.890625).astype(jnp.bfloat16),
        "courant_y": jnp.clip(0.099609375 + 2.7910156 * jax.random.uniform(streams_of[2], (WINDOWS, TILES, LEV, SIDE * SIDE), jnp.float32) ** shard_levels(streams_of[2], (WINDOWS, TILES, LEV, SIDE * SIDE), ((0, 4), (1, 64)), -0.2, 0.2), 0.099609375, 2.890625).astype(jnp.bfloat16),
        "observed": bell_draw(streams_of[3], (WINDOWS, TILES, SIDE, SIDE), 0.5, 3.0, ((0, 4), (1, 64)), jnp.float32),
        "precision_w": jnp.clip(jnp.exp(math.log(2.0) - 2.3025851 * jax.random.uniform(streams_of[4], (WINDOWS, TILES, SIDE, SIDE), jnp.float32) ** shard_levels(streams_of[4], (WINDOWS, TILES, SIDE, SIDE), ((0, 4), (1, 64)), -0.2, 0.2)), 0.2, 2.0),
        "kernel": jnp.clip(jnp.exp(jax.random.uniform(streams_of[5], (LEV,), jnp.float32, math.log(0.1), math.log(1.0))), 0.1, 1.0),
        "profile": jnp.clip(jnp.exp(jax.random.uniform(streams_of[6], (LEV,), jnp.float32, math.log(0.05), math.log(1.0))), 0.05, 1.0),
        "emission": bell_draw(streams_of[7], (TILES, SIDE, SIDE), 1.0, 6.0, ((0, 64),), jnp.float32),
        "edges": draw_edges(jax.random.fold_in(streams_of[9], 71), 0),
    }


def advect_along(tracer_field, rim_cells, courant, along):
    side_len = tracer_field.shape[along]
    extended = jnp.concatenate([rim_cells, tracer_field], along)
    edge_speed = lax.slice_in_dim(courant, side_len - 1, side_len, axis=along)
    inflow = jnp.zeros_like(tracer_field)
    outlet = jnp.zeros_like(edge_speed)
    for depth in range(1, 4):
        inflow = inflow + lax.slice_in_dim(extended, 3 - depth, 3 - depth + side_len, axis=along) * jnp.clip(courant - (depth - 1), 0.0, 1.0)
        outlet = outlet + lax.slice_in_dim(tracer_field, side_len - depth, side_len - depth + 1, axis=along) * jnp.clip(edge_speed - (depth - 1), 0.0, 1.0)
    outflow = jnp.concatenate([lax.slice_in_dim(inflow, 1, side_len, axis=along), outlet], along)
    return tracer_field - (outflow - inflow)

def strips(tracer_field):
    side_len = tracer_field.shape[-1]
    east_strip = jnp.swapaxes(tracer_field[..., side_len - 3:][..., ::-1], -1, -2)
    north_strip = tracer_field[..., side_len - 3:, :][..., ::-1, :]
    return (east_strip, north_strip)

def as_halo(panel, along):
    if along == 3:
        return jnp.swapaxes(panel[..., ::-1, :], -1, -2)
    return panel[..., ::-1, :]

def halo_from(tracer_field, source_tile, edge_code, flip_code, along):
    east_strip, north_strip = strips(tracer_field)
    chosen = jnp.where((edge_code == 0)[:, None, None, None], east_strip[source_tile], north_strip[source_tile])
    chosen = jnp.where((flip_code == 1)[:, None, None, None], chosen[..., ::-1], chosen)
    return as_halo(chosen, along)

def window_cost(emission, initial_field, speed_x, speed_y, observed_w, weights, kernel, profile, edges):
    tracer_field = initial_field
    for step_index in range(STEPS):
        tracer_field = advect_along(tracer_field, halo_from(tracer_field, edges[0], edges[1], edges[2], 3), speed_x, 3)
        tracer_field = advect_along(tracer_field, halo_from(tracer_field, edges[3], edges[4], edges[5], 2), speed_y, 2)
        tracer_field = tracer_field + profile[None, :, None, None] * emission[:, None]
    column = lax.optimization_barrier(jnp.sum(kernel[None, :, None, None] * tracer_field, axis=1)) / jnp.sum(kernel)
    misfit = column - observed_w
    return 0.5 * jnp.sum(weights * misfit * misfit)

def reference(initial, courant_x, courant_y, observed, precision_w, kernel, profile, emission, edges):

    def per_window(running, window_items):
        initial_field, speed_x, speed_y, observed_w, weights = window_items
        cube_shape = (TILES, LEV, SIDE, SIDE)
        window_grad = jax.grad(window_cost)(emission, initial_field.reshape(cube_shape), speed_x.astype(jnp.float32).reshape(cube_shape), speed_y.astype(jnp.float32).reshape(cube_shape), observed_w, weights, kernel, profile, edges)
        return (running + window_grad, None)
    running, unused = lax.scan(per_window, jnp.zeros_like(emission), (initial, courant_x, courant_y, observed, precision_w))
    return running
```

```python
import jax
import jax.numpy as jnp
from jax import lax
from jax.experimental import pallas as pl
from jax.experimental.pallas import tpu as pltpu
from jax.sharding import PartitionSpec as P

F32 = jnp.float32
BF16 = jnp.bfloat16
I32 = jnp.int32
SIDE = 64
LANES = 128
CELLS = SIDE * SIDE
NV = CELLS // LANES
MESH = pl.DeviceIdType.MESH


def roll(x, shift):
    return pltpu.roll(x, shift % LANES, 1)


def lanes_of(shape):
    return lax.broadcasted_iota(I32, shape, 1)


def coefs(c):
    return jnp.clip(c, 0.0, 1.0), jnp.clip(c - 1.0, 0.0, 1.0), jnp.clip(c - 2.0, 0.0, 1.0)


def chunk(v):
    if isinstance(v, int):
        return pl.ds(v * LANES, LANES)
    return pl.ds(pl.multiple_of(v * LANES, LANES), LANES)


def slot_key(index):
    part = index & 3
    cell = 32 * (index >> 7) + 2 * ((index >> 2) & 15) + ((index >> 6) & 1)
    return part * SIDE + cell, part < 3


def north_key(index):
    return index - SIDE, index >= SIDE


def make_kernel(levels, windows):
    rows = (levels + 7) // 8 * 8
    per = NV // windows

    def kernel(
        init_h, cx_h, cy_h, obs_h, pre_h, ker_h, pro_h, emi_h, edges,
        out,
        qi, q, bx, mu, cx, cy, cxb, cyb, sq, sq2, flat, kp, kcol, pcol, gf,
        wx, wxt, wy, wyt, epack, cpack, dbuf,
        sbuf, rbuf, sset, rset, scol, rcol, spb, rpb, gint, rg, fin,
        in_sem, s_sem, r_sem, sset_sem, rset_sem, scol_sem, rcol_sem, spb_sem, rpb_sem, sg_sem, rg_sem,
    ):
        w = lax.axis_index("win")
        t = lax.axis_index("tile")
        tiles = lax.axis_size("tile")
        off_x = (1, tiles // 4)
        off_y = (2, tiles // 2)

        def fwd(off):
            return lax.rem(t + off, tiles)

        def bwd(off):
            return lax.rem(t + tiles - off, tiles)

        def win_of(r):
            return lax.rem(w + r, windows)

        loads = [
            pltpu.make_async_copy(init_h, qi, in_sem.at[0]),
            pltpu.make_async_copy(cx_h.at[0, 0], cxb, in_sem.at[1]),
            pltpu.make_async_copy(cy_h.at[0, 0], cyb, in_sem.at[2]),
            pltpu.make_async_copy(ker_h, kp.at[0], in_sem.at[3]),
            pltpu.make_async_copy(pro_h, kp.at[1], in_sem.at[4]),
            pltpu.make_async_copy(emi_h.at[0], sq.at[0], in_sem.at[5]),
            pltpu.make_async_copy(obs_h.at[0, 0], sq.at[1], in_sem.at[6]),
            pltpu.make_async_copy(pre_h.at[0, 0], sq.at[2], in_sem.at[7]),
        ]
        for load in loads:
            load.start()

        barrier = pltpu.get_barrier_semaphore()
        partners = []
        near = {1, tiles // 4, tiles - 1, tiles - tiles // 4}
        far = near | {2, tiles - 2, tiles // 2}
        for off in sorted(far):
            partners.append((w, fwd(off)))
        for r in range(1, windows):
            for off in sorted(near | {0}):
                partners.append((win_of(r), fwd(off)))
        for who in partners:
            pl.semaphore_signal(barrier, inc=1, device_id=who, device_id_type=MESH)

        lane = lanes_of((rows, LANES))
        l64 = lane & (SIDE - 1)
        low = lane < SIDE
        lane8 = lanes_of((8, LANES))
        l64_8 = lane8 & (SIDE - 1)
        low8 = lane8 < SIDE
        lane1 = lanes_of((1, LANES))
        low1 = lane1 < SIDE

        row_index = lax.broadcasted_iota(I32, (256, LANES), 0)

        def rows_key(kind):
            key, valid = (slot_key if kind == 0 else north_key)(row_index)
            return jnp.where(valid, key, -1000)

        def cols_key(kind, half):
            key, valid = (slot_key if kind == 0 else north_key)(lane1 + half * LANES)
            return jnp.where(valid, key, -2000)

        def choices(base, offs):
            out_ = []
            for off in offs:
                to = fwd(off)
                mine = (edges[base, to] == t).astype(I32)
                code = edges[base + 1, to]
                flip = edges[base + 2, to]
                out_.append((63 * flip, 4096 * (1 - mine * (1 - code)), 4096 * (1 - mine * code)))
            return out_

        row_keys = (rows_key(0), rows_key(1))

        def hot(mask):
            return jnp.where(mask, 1.0, 0.0).astype(BF16)

        def build(mat, base, offs, kind, transposed):
            for d, (flip, not_east, not_north) in enumerate(choices(base, offs)):
                for src in range(2):
                    away = not_east if src == 0 else not_north
                    for half in range(2):
                        if transposed:
                            cols = (cols_key(src, half) ^ flip) + away
                            mat[pl.ds(d * 256, 256), pl.ds(src * 256 + half * LANES, LANES)] = hot(row_keys[kind] == cols)
                        else:
                            cols = (cols_key(kind, half) ^ flip) + away
                            mat[pl.ds(src * 256, 256), pl.ds(d * 256 + half * LANES, LANES)] = hot(row_keys[src] == cols)

        def permute(x, mat):
            top = x.astype(BF16).astype(F32)
            both = jnp.concatenate([top, x - top], axis=0).astype(BF16)
            res = jnp.dot(both, mat[...], preferred_element_type=F32)
            n = x.shape[0]
            return res[:n] + res[n:]

        def send(stage, d, to):
            copy = pltpu.make_async_remote_copy(
                src_ref=sbuf.at[stage, d], dst_ref=rbuf.at[stage, d],
                send_sem=s_sem.at[stage, d], recv_sem=r_sem.at[stage, d],
                device_id=(w, to), device_id_type=MESH,
            )
            copy.start()
            return copy

        pending = []

        def send_strips(stage, east, north, mat, offs):
            res = permute(jnp.concatenate([east, north], axis=1), mat)
            copies = []
            for d in range(2):
                sbuf[stage, d] = res[:, d * 256 : (d + 1) * 256]
            for d in range(2):
                copies.append(send(stage, d, fwd(offs[d])))
            pending.extend(copies)
            return copies

        def received(copies, stage):
            for copy in copies:
                copy.wait_recv()
            return rbuf[stage, 0] + rbuf[stage, 1]

        def pack_into(dst, src, v, first, pad):
            g, u = v // 16, v % 16
            moved = roll(src[:, chunk(v + pad)], 4 * u - first)
            take = ((l64 >> 2) == u) & ((l64 & 3) < 3)
            here = pl.ds(g * LANES, LANES)
            dst[:, here] = jnp.where(take, moved, dst[:, here])

        def pack_group(src, g, first, pad, us, start):
            acc = start
            for u in us:
                moved = roll(src[:, chunk(16 * g + u + pad)], 4 * u - first)
                acc = jnp.where(((l64 >> 2) == u) & ((l64 & 3) < 3), moved, acc)
            return acc

        def pack(dst, src, first, pad):
            for g in range(2):
                dst[:, pl.ds(g * LANES, LANES)] = pack_group(src, g, first, pad, range(16), jnp.zeros((rows, LANES), F32))

        build(wx, 0, off_x, 0, False)
        q[pl.ds(levels, rows - levels), :] = jnp.zeros((rows - levels, CELLS), F32)
        loads[0].wait()

        @pl.loop(0, NV)
        def _(v):
            q[pl.ds(0, levels), chunk(v)] = qi[pl.ds(v, levels, stride=NV), :]

        pack(epack, q, 61, 0)
        strips = permute(jnp.concatenate([epack[...], q[:, pl.ds(CELLS - 256, 256)]], axis=1), wx)
        for d in range(2):
            sbuf[0, d] = strips[:, d * 256 : (d + 1) * 256]
        pl.semaphore_wait(barrier, len(partners))
        first = [send(0, d, fwd(off_x[d])) for d in range(2)]
        pending.extend(first)

        loads[1].wait()
        loads[2].wait()
        for c, cb in ((cx, cxb), (cy, cyb)):
            c[pl.ds(levels, rows - levels), :] = jnp.zeros((rows - levels, CELLS), F32)

            @pl.loop(0, NV)
            def _(v, c=c, cb=cb):
                c[pl.ds(0, levels), chunk(v)] = cb[:, chunk(v)].astype(F32)

        def x_interior():
            @pl.loop(0, NV)
            def _(v):
                here = q[:, chunk(v)]
                a1, a2, a3 = coefs(cx[:, chunk(v)])
                r1, r2, r3 = roll(here, 1), roll(here, 2), roll(here, 3)
                flux = (
                    jnp.where(l64 >= 1, r1, 0.0) * a1
                    + jnp.where(l64 >= 2, r2, 0.0) * a2
                    + jnp.where(l64 >= 3, r3, 0.0) * a3
                )
                outlet = here * a1 + r1 * a2 + r2 * a3
                bx[:, chunk(v + 2)] = here + flux - jnp.where(l64 == SIDE - 1, outlet, roll(flux, -1))

        x_interior()

        for i in range(3):
            loads[5 + i].wait()
            x = sq[i]
            sq2[i, :, pl.ds(0, SIDE)] = x

        for i in range(3):
            x = sq2[i]
            sq2[i] = jnp.where(lanes_of((SIDE, LANES)) < SIDE, x, pltpu.roll(x, SIDE, 1))

        for i in range(3):
            @pl.loop(0, NV)
            def _(v, i=i):
                row = jnp.where(low1, sq2[i, pl.ds(2 * v, 1), :], sq2[i, pl.ds(2 * v + 1, 1), :])
                flat[i, :, chunk(v)] = jnp.broadcast_to(row, (8, LANES))

        loads[3].wait()
        loads[4].wait()
        diag = lax.broadcasted_iota(I32, (levels, levels), 0) == lax.broadcasted_iota(I32, (levels, levels), 1)
        for i, col in ((0, kcol), (1, pcol)):
            column = jnp.sum(jnp.where(diag, jnp.broadcast_to(kp[i], (levels, levels)), 0.0), axis=1, keepdims=True)
            col[...] = jnp.zeros((rows, LANES), F32)
            col[pl.ds(0, levels), :] = jnp.broadcast_to(column, (levels, LANES))
        inv = 1.0 / jnp.sum(kp[0], axis=1, keepdims=True)
        inv8 = jnp.broadcast_to(inv, (8, LANES))

        sset[pl.ds(0, rows), :] = cy[:, pl.ds(0, 256)]
        for i in range(2):
            sset[pl.ds(rows + 8 * i, 8), :] = flat[1 + i, :, pl.ds(0, 256)]
        sets = []
        for d in range(2):
            copy = pltpu.make_async_remote_copy(
                src_ref=sset, dst_ref=rset.at[d], send_sem=sset_sem.at[d], recv_sem=rset_sem.at[d],
                device_id=(w, bwd(off_y[d])), device_id_type=MESH,
            )
            copy.start()
            sets.append(copy)

        build(wy, 3, off_y, 1, False)

        pack(cpack, cx, 0, 0)
        part = lanes_of((rows, 256)) & 3
        p1, p2, p3 = coefs(cpack[...])
        west1 = jnp.where(part == 0, p1, 0.0)
        west2 = jnp.where(part <= 1, p2, 0.0)
        west3 = jnp.where(part <= 2, p3, 0.0)
        cpack3 = (west1, west2, west3)

        def roll2(x, shift):
            return jnp.concatenate([roll(x[:, :LANES], shift), roll(x[:, LANES:], shift)], axis=1)

        def west_change(panel):
            f = panel * cpack3[2] + roll2(panel, -1) * cpack3[1] + roll2(panel, -2) * cpack3[0]
            return jnp.where(part < 3, f - roll2(f, -1), 0.0)

        def unpacked(src, g, u, first, mask):
            return jnp.where(mask, roll(src[:, g * LANES : (g + 1) * LANES], first - 4 * u), 0.0)

        def add_west(v):
            bx[:, chunk(v + 2)] = bx[:, chunk(v + 2)] + unpacked(dbuf, v // 16, v % 16, 0, l64 < 3)

        def y_flux(qv_r, q1, q1_r, q2_r, c):
            a1, a2, a3 = coefs(c)
            s1 = jnp.where(low, q1_r, qv_r)
            return s1 * a1 + q1 * a2 + jnp.where(low, q2_r, q1_r) * a3

        def y_start():
            q31, q30 = bx[:, chunk(NV + 1)], bx[:, chunk(NV)]
            r31, r30 = roll(q31, SIDE), roll(q30, SIDE)
            a1, a2, a3 = coefs(cy[:, chunk(NV - 1)])
            outlet = q31 * a1 + jnp.where(low, r30, r31) * a2 + q30 * a3
            return q31, r31, q30, r30, outlet

        def y_step(v, carry):
            qv, rv, q1, r1, above = carry
            q2 = bx[:, chunk(v)]
            r2 = roll(q2, SIDE)
            flux = y_flux(rv, q1, r1, r2, cy[:, chunk(v)])
            turned = roll(flux, SIDE)
            return qv + flux - jnp.where(low, turned, above), (q1, r1, q2, r2, turned)

        def emitted(v):
            return pcol[...] * jnp.concatenate([flat[0, :, chunk(v)]] * (rows // 8), axis=0)

        def sum_levels(x, col):
            x = x * col
            acc = x[0:8]
            for i in range(1, rows // 8):
                acc = acc + x[8 * i : 8 * i + 8]
            return acc

        def down(x):
            return jnp.broadcast_to(jnp.sum(x, axis=0, keepdims=True), (8, LANES))

        def tall(x):
            return jnp.concatenate([x] * (rows // 8), axis=0)

        pack(epack, bx, 61, 2)
        panel = received(first, 0)
        dbuf[...] = west_change(panel)
        add_west(NV - 2)
        add_west(NV - 1)
        y1 = send_strips(1, epack[...], bx[:, pl.ds(CELLS, 256)], wy, off_y)
        for v in range(NV - 2):
            add_west(v)

        def forward(v, carry):
            res, carry = y_step(v, carry)
            q[:, chunk(v)] = res + emitted(v)
            return carry

        carry = lax.fori_loop(0, NV - 2, lambda i, carry: forward(NV - 1 - i, carry), y_start())
        epack[:, pl.ds(0, LANES)] = pack_group(q, 0, 61, 0, range(2, 16), jnp.zeros((rows, LANES), F32))
        epack[:, pl.ds(LANES, LANES)] = pack_group(q, 1, 61, 0, range(16), jnp.zeros((rows, LANES), F32))

        bx[:, pl.ds(0, 256)] = received(y1, 1)
        for v in (1, 0):
            carry = forward(v, carry)
        epack[:, pl.ds(0, LANES)] = pack_group(q, 0, 61, 0, range(2), epack[:, pl.ds(0, LANES)])

        x2 = send_strips(2, epack[...], q[:, pl.ds(CELLS - 256, 256)], wx, off_x)
        x_interior()
        pack(epack, bx, 61, 2)
        build(wyt, 3, off_y, 1, True)
        for copy in sets:
            copy.wait_recv()

        panel = received(x2, 2)
        dbuf[...] = west_change(panel)
        add_west(NV - 2)
        add_west(NV - 1)
        y2 = send_strips(3, epack[...], bx[:, pl.ds(CELLS, 256)], wy, off_y)
        for v in range(NV - 2):
            add_west(v)

        def misfit_weight(col, v_obs, v_pre):
            return v_pre * (col * inv8 - v_obs) * inv8

        k_all = kcol[...]
        zero = jnp.zeros((rows, LANES), F32)
        q0_, q1_, q2_ = bx[:, chunk(2)], bx[:, chunk(3)], bx[:, chunk(4)]
        t0, t1, t2 = roll(q0_, SIDE), roll(q1_, SIDE), roll(q2_, SIDE)
        above = roll(y_flux(t2, q1_, t1, t0, cy[:, chunk(2)]), SIDE)
        f1 = y_flux(t1, q0_, t0, zero, cy[:, chunk(1)])
        f0 = y_flux(t0, zero, zero, zero, cy[:, chunk(0)])
        g1, g0 = roll(f1, SIDE), roll(f0, SIDE)
        n1 = q1_ + f1 - jnp.where(low, g1, above) + emitted(1)
        n0 = q0_ + f0 - jnp.where(low, g0, g1) + emitted(0)
        for v, n in ((0, n0), (1, n1)):
            scol[:, chunk(v)] = down(sum_levels(n, k_all))
        cols = []
        for d in range(2):
            copy = pltpu.make_async_remote_copy(
                src_ref=scol, dst_ref=rcol.at[d], send_sem=scol_sem.at[d], recv_sem=rcol_sem.at[d],
                device_id=(w, bwd(off_y[d])), device_id_type=MESH,
            )
            copy.start()
            cols.append(copy)

        def last(v, carry):
            res, carry = y_step(v, carry)
            col = down(sum_levels(res + emitted(v), k_all))
            gf[:, chunk(v)] = misfit_weight(col, flat[1, :, chunk(v)], flat[2, :, chunk(v)])
            return carry

        carry = lax.fori_loop(0, NV - 2, lambda i, carry: last(NV - 1 - i, carry), y_start())

        def terms(v, below):
            here = gf[:, chunk(v)]
            diff = here - jnp.where(low8, roll(below, SIDE), roll(here, SIDE))
            bar = k_all * tall(diff)
            a1, a2, a3 = coefs(cy[:, chunk(v)])
            return bar * a1, bar * a2, bar * a3

        def up_step(v, made, carry):
            first_above, second_above, third_above, third_above2 = carry
            m1, m2, m3 = made
            turned1, turned3 = roll(m1, SIDE), roll(m3, SIDE)
            res = (
                k_all * tall(gf[:, chunk(v)])
                + jnp.where(low, turned1, first_above)
                + second_above
                + jnp.where(low, third_above, third_above2)
            )
            mu[:, chunk(v)] = res
            return turned1, m2, turned3, third_above

        gf[:, chunk(0)] = jnp.zeros((8, LANES), F32)
        gf[:, chunk(1)] = jnp.zeros((8, LANES), F32)
        top = -k_all * tall(roll(gf[:, chunk(NV - 1)], SIDE))
        b1, b2, b3 = coefs(roll(cy[:, chunk(NV - 1)], SIDE))
        e1 = jnp.where(low, top * b1, 0.0)
        e2 = jnp.where(low, top * b2, 0.0)
        e3 = jnp.where(low, top * b3, 0.0)
        start = (roll(e1, SIDE), e2, roll(e3, SIDE), zero)

        def climb(i, state):
            v = NV - 1 - i
            made = terms(v, gf[:, chunk(v - 1)])
            return up_step(v, made, state)

        state3 = lax.fori_loop(0, NV - 3, climb, start)
        state2 = up_step(2, terms(2, gf[:, chunk(1)]), state3)

        dbuf[:, pl.ds(0, LANES)] = pack_group(mu, 0, 0, 0, range(2, 16), zero)
        dbuf[:, pl.ds(LANES, LANES)] = pack_group(mu, 1, 0, 0, range(14), zero)
        build(wxt, 0, off_x, 0, True)

        bars = []
        for d in range(2):
            cols[d].wait_recv()
            pa, pb = sbuf[3, d, :, pl.ds(0, LANES)], sbuf[3, d, :, pl.ds(LANES, LANES)]
            ra, rb = roll(pa, SIDE), roll(pb, SIDE)
            c0, c1 = rset[d, pl.ds(0, rows), pl.ds(0, LANES)], rset[d, pl.ds(0, rows), pl.ds(LANES, LANES)]
            z1, z2, z3 = coefs(c0)
            o1, o2, o3 = coefs(c1)
            h0 = jnp.where(low, rb, 0.0) * z1 + pb * z2 + jnp.where(low, ra, rb) * z3
            h1 = jnp.where(low, rb, 0.0) * o3
            k0, k1 = roll(h0, SIDE), roll(h1, SIDE)
            d0 = h0 - jnp.where(low, k0, k1)
            d1 = h1 - jnp.where(low, k1, 0.0)
            w0 = misfit_weight(
                rcol[d, :, chunk(0)] + down(sum_levels(d0, k_all)),
                rset[d, pl.ds(rows, 8), chunk(0)], rset[d, pl.ds(rows + 8, 8), chunk(0)],
            )
            w1 = misfit_weight(
                rcol[d, :, chunk(1)] + down(sum_levels(d1, k_all)),
                rset[d, pl.ds(rows, 8), chunk(1)], rset[d, pl.ds(rows + 8, 8), chunk(1)],
            )
            turned = roll(w0, SIDE)
            bar0 = k_all * tall(w0 - jnp.where(low8, 0.0, turned))
            bar1 = k_all * tall(w1 - jnp.where(low8, turned, roll(w1, SIDE)))
            third0, third1 = roll(bar0 * z3, SIDE), roll(bar1 * o3, SIDE)
            near_rows = jnp.where(low, 0.0, roll(bar0 * z1, SIDE)) + bar0 * z2 + jnp.where(low, third0, third1)
            far_rows = jnp.where(low, 0.0, third0)
            bars.append(jnp.concatenate([far_rows, near_rows], axis=1))
        back = permute(jnp.concatenate(bars, axis=1), wyt)
        back_east, back_north = back[:, :256], back[:, 256:]

        bx[:, pl.ds(0, 256)] = received(y2, 3)
        for v in (1, 0):
            carry = last(v, carry)
        state = up_step(2, terms(2, gf[:, chunk(1)]), state3)
        state = up_step(1, terms(1, gf[:, chunk(0)]), state)
        state = up_step(0, terms(0, jnp.zeros((8, LANES), F32)), state)
        mu[:, pl.ds(CELLS - 256, 256)] = mu[:, pl.ds(CELLS - 256, 256)] + back_north
        west0 = pack_group(mu, 0, 0, 0, range(2), dbuf[:, pl.ds(0, LANES)])
        west1_ = pack_group(mu, 1, 0, 0, range(14, 16), dbuf[:, pl.ds(LANES, LANES)])
        west = jnp.concatenate([west0, west1_], axis=1)
        diff = west - jnp.where(part > 0, roll2(west, 1), 0.0)
        pbar = diff * cpack3[2] + roll2(diff * cpack3[1], 1) + roll2(diff * cpack3[0], 2)
        p_all = pcol[...]
        for v in range(2):
            spb[:, chunk(v)] = down(sum_levels(pbar[:, v * LANES : (v + 1) * LANES], p_all))
        finals = []
        for r in range(windows):
            for d in range(2):
                copy = pltpu.make_async_remote_copy(
                    src_ref=spb, dst_ref=rpb.at[d, r], send_sem=spb_sem.at[d, r], recv_sem=rpb_sem.at[d, r],
                    device_id=(win_of(r), bwd(off_x[d])), device_id_type=MESH,
                )
                copy.start()
                finals.append(copy)

        for v in range(NV):
            mu[:, chunk(v)] = mu[:, chunk(v)] + unpacked(back_east, v // 16, v % 16, 61, l64 >= 61)
        both = jnp.broadcast_to(jnp.sum(kcol[...] * pcol[...], axis=0, keepdims=True), (8, LANES))

        @pl.loop(0, NV)
        def _(v):
            m = mu[:, chunk(v)] * p_all
            a1, a2, a3 = coefs(cx[:, chunk(v)])
            f = m - jnp.where(l64 >= 1, roll(m, 1), 0.0)
            ones = jnp.ones((rows, LANES), F32)
            s0 = sum_levels(m, ones)
            s1, s2, s3 = sum_levels(f * a1, ones), sum_levels(f * a2, ones), sum_levels(f * a3, ones)
            z1, z2, z3 = sum_levels(m * a1, ones), sum_levels(m * a2, ones), sum_levels(m * a3, ones)
            res = s0 + jnp.where(l64_8 < 63, roll(s1, -1), -z1)
            res = res + jnp.where(l64_8 < 62, roll(s2, -2), jnp.where(l64_8 == 62, -roll(z2, -1), 0.0))
            res = res + jnp.where(l64_8 < 61, roll(s3, -3), jnp.where(l64_8 == 61, -roll(z3, -2), 0.0))
            gint[pl.ds(v, 1), :] = (down(res) + both * gf[:, chunk(v)])[0:1]

        sums = []
        for r in range(1, windows):
            to = win_of(r)
            copy = pltpu.make_async_remote_copy(
                src_ref=gint.at[pl.ds(pl.multiple_of(to * per, per), per), :], dst_ref=rg.at[r - 1],
                send_sem=sg_sem.at[r - 1], recv_sem=rg_sem.at[r - 1],
                device_id=(to, t), device_id_type=MESH,
            )
            copy.start()
            sums.append(copy)

        for copy in finals:
            copy.wait_recv()
        halves = []
        for d in range(2):
            acc = rpb[d, 0]
            for r in range(1, windows):
                acc = acc + rpb[d, r]
            halves.append(acc)
        ends = permute(jnp.concatenate(halves, axis=1), wxt)
        for v in range(NV):
            g, u = v // 16, v % 16
            row = jnp.where(l64_8 >= 61, roll(ends[:, g * LANES : (g + 1) * LANES], 61 - 4 * u), 0.0)
            if v >= NV - 2:
                at = 256 + (v - NV + 2) * LANES
                row = row + ends[:, at : at + LANES]
            fin[pl.ds(v, 1), :] = row[0:1]
        mine = pl.ds(pl.multiple_of(w * per, per), per)
        total = gint[mine, :] + fin[mine, :]
        for copy in sums:
            copy.wait_recv()
        for r in range(1, windows):
            total = total + rg[r - 1]
        out[0, pl.ds(0, per, stride=2), :] = total[:, :SIDE]
        out[0, pl.ds(1, per, stride=2), :] = pltpu.roll(total, SIDE, 1)[:, :SIDE]

        for copy in pending + sets + cols + finals + sums:
            copy.wait_send()

    return kernel, rows, per


def body(initial, courant_x, courant_y, observed, precision_w, kernel, profile, emission, edges):
    levels = initial.shape[2]
    windows = lax.axis_size("win")
    run, rows, per = make_kernel(levels, windows)
    vm = pltpu.VMEM
    dma = pltpu.SemaphoreType.DMA
    anywhere = pl.BlockSpec(memory_space=pl.ANY)
    return pl.pallas_call(
        run,
        out_shape=jax.ShapeDtypeStruct((1, 2 * per, SIDE), F32),
        in_specs=[anywhere] * 8 + [pl.BlockSpec(memory_space=pltpu.SMEM)],
        out_specs=pl.BlockSpec(memory_space=pltpu.VMEM),
        scratch_shapes=[
            vm((levels * NV, LANES), F32),
            vm((rows, CELLS), F32),
            vm((rows, CELLS + 256), F32),
            vm((rows, CELLS), F32),
            vm((rows, CELLS), F32),
            vm((rows, CELLS), F32),
            vm((levels, CELLS), BF16),
            vm((levels, CELLS), BF16),
            vm((3, SIDE, SIDE), F32),
            vm((3, SIDE, LANES), F32),
            vm((3, 8, CELLS), F32),
            vm((2, 1, levels), F32),
            vm((rows, LANES), F32),
            vm((rows, LANES), F32),
            vm((8, CELLS), F32),
            vm((512, 512), BF16),
            vm((512, 512), BF16),
            vm((512, 512), BF16),
            vm((512, 512), BF16),
            vm((rows, 256), F32),
            vm((rows, 256), F32),
            vm((rows, 256), F32),
            vm((4, 2, rows, 256), F32),
            vm((4, 2, rows, 256), F32),
            vm((rows + 16, 256), F32),
            vm((2, rows + 16, 256), F32),
            vm((8, 256), F32),
            vm((2, 8, 256), F32),
            vm((8, 256), F32),
            vm((2, windows, 8, 256), F32),
            vm((NV, LANES), F32),
            vm((windows - 1, per, LANES), F32),
            vm((NV, LANES), F32),
            dma((8,)),
            dma((4, 2)),
            dma((4, 2)),
            dma((2,)),
            dma((2,)),
            dma((2,)),
            dma((2,)),
            dma((2, windows)),
            dma((2, windows)),
            dma((windows - 1,)),
            dma((windows - 1,)),
        ],
        compiler_params=pltpu.CompilerParams(collective_id=0, has_side_effects=True),
    )(
        initial.reshape(levels * NV, LANES), courant_x, courant_y, observed, precision_w,
        kernel.reshape(1, levels), profile.reshape(1, levels), emission, edges,
    )


def solution(mesh):
    placed = (
        P("win", "tile", None, None),
        P("win", "tile", None, None),
        P("win", "tile", None, None),
        P("win", "tile", None, None),
        P("win", "tile", None, None),
        P(),
        P(),
        P("tile", None, None),
        P(),
    )
    return jax.shard_map(
        body, mesh=mesh, in_specs=placed, out_specs=P("tile", "win", None), check_vma=False
    )
```

```python
import jax
import jax.numpy as jnp
from jax import lax
from jax.experimental import pallas as pl
from jax.experimental.pallas import tpu as pltpu
from jax.sharding import PartitionSpec as P

F32 = jnp.float32
BF16 = jnp.bfloat16
I32 = jnp.int32
SIDE = 64
LANES = 128
CELLS = SIDE * SIDE
NV = CELLS // LANES
MESH = pl.DeviceIdType.MESH


def roll(x, shift):
    return pltpu.roll(x, shift % LANES, 1)


def lanes_of(shape):
    return lax.broadcasted_iota(I32, shape, 1)


def coefs(c):
    one, three = jnp.minimum(c, 1.0), jnp.maximum(c - 2.0, 0.0)
    return one, c - one - three, three


def chunk(v):
    if isinstance(v, int):
        return pl.ds(v * LANES, LANES)
    return pl.ds(pl.multiple_of(v * LANES, LANES), LANES)


def slot_key(index):
    part = index & 3
    cell = 32 * (index >> 7) + 2 * ((index >> 2) & 15) + ((index >> 6) & 1)
    return part * SIDE + cell, part < 3


def north_key(index):
    return index - SIDE, index >= SIDE


def make_kernel(levels, windows):
    rows = (levels + 7) // 8 * 8
    per = NV // windows

    def kernel(
        init_h, cx_h, cy_h, obs_h, pre_h, ker_h, pro_h, emi_h, edges,
        out,
        qi, q, bx, mu, cx, cy, cxb, cyb, sq, sq2, flat, kp, kcol, pcol, gf, df, bfix,
        wx, wxt, wy, wyt, epack, ewrap, cpack, dbuf,
        sbuf, rbuf, sset, rset, scol, rcol, spb, rpb, gint, rg, fin,
        in_sem, s_sem, r_sem, sset_sem, rset_sem, scol_sem, rcol_sem, spb_sem, rpb_sem, sg_sem, rg_sem,
    ):
        w = lax.axis_index("win")
        t = lax.axis_index("tile")
        tiles = lax.axis_size("tile")
        off_x = (1, tiles // 4)
        off_y = (2, tiles // 2)

        def fwd(off):
            return lax.rem(t + off, tiles)

        def bwd(off):
            return lax.rem(t + tiles - off, tiles)

        def win_of(r):
            return lax.rem(w + r, windows)

        loads = [
            pltpu.make_async_copy(cx_h.at[0, 0], cxb, in_sem.at[0]),
            pltpu.make_async_copy(cy_h.at[0, 0], cyb, in_sem.at[1]),
            pltpu.make_async_copy(ker_h, kp.at[0], in_sem.at[2]),
            pltpu.make_async_copy(pro_h, kp.at[1], in_sem.at[3]),
            pltpu.make_async_copy(emi_h.at[0], sq.at[0], in_sem.at[4]),
            pltpu.make_async_copy(obs_h.at[0, 0], sq.at[1], in_sem.at[5]),
            pltpu.make_async_copy(pre_h.at[0, 0], sq.at[2], in_sem.at[6]),
        ]
        tiles_of = rows // 8
        fields = []
        for i in range(tiles_of):
            some = pl.ds(8 * NV * i, NV * min(8, levels - 8 * i))
            fields.append(pltpu.make_async_copy(init_h.at[some, :], qi.at[some, :], in_sem.at[7 + i]))
        for load in fields + loads:
            load.start()

        barrier = pltpu.get_barrier_semaphore()
        partners = []
        near = {1, tiles // 4, tiles - 1, tiles - tiles // 4}
        far = near | {2, tiles - 2, tiles // 2}
        for off in sorted(far):
            partners.append((w, fwd(off)))
        for r in range(1, windows):
            for off in sorted(near | {0}):
                partners.append((win_of(r), fwd(off)))
        for who in partners:
            pl.semaphore_signal(barrier, inc=1, device_id=who, device_id_type=MESH)

        lane = lanes_of((rows, LANES))
        l64 = lane & (SIDE - 1)
        low = lane < SIDE
        lane8 = lanes_of((8, LANES))
        l64_8 = lane8 & (SIDE - 1)
        low8 = lane8 < SIDE
        lane1 = lanes_of((1, LANES))
        low1 = lane1 < SIDE

        row_index = lax.broadcasted_iota(I32, (256, LANES), 0)

        def rows_key(kind):
            key, valid = (slot_key if kind == 0 else north_key)(row_index)
            return jnp.where(valid, key, -1000)

        def cols_key(kind, half):
            key, valid = (slot_key if kind == 0 else north_key)(lane1 + half * LANES)
            return jnp.where(valid, key, -2000)

        def choices(base, offs):
            out_ = []
            for off in offs:
                to = fwd(off)
                mine = (edges[base, to] == t).astype(I32)
                code = edges[base + 1, to]
                flip = edges[base + 2, to]
                out_.append((63 * flip, 4096 * (1 - mine * (1 - code)), 4096 * (1 - mine * code)))
            return out_

        row_keys = (rows_key(0), rows_key(1))

        def hot(mask):
            return jnp.where(mask, 1.0, 0.0).astype(BF16)

        def build(mat, base, offs, kind, transposed):
            for d, (flip, not_east, not_north) in enumerate(choices(base, offs)):
                for src in range(2):
                    away = not_east if src == 0 else not_north
                    for half in range(2):
                        if transposed:
                            cols = (cols_key(src, half) ^ flip) + away
                            mat[pl.ds(d * 256, 256), pl.ds(src * 256 + half * LANES, LANES)] = hot(row_keys[kind] == cols)
                        else:
                            cols = (cols_key(kind, half) ^ flip) + away
                            mat[pl.ds(src * 256, 256), pl.ds(d * 256 + half * LANES, LANES)] = hot(row_keys[src] == cols)

        def permute(x, mat):
            top = x.astype(BF16).astype(F32)
            both = jnp.concatenate([top, x - top], axis=0).astype(BF16)
            res = jnp.dot(both, mat[...], preferred_element_type=F32)
            n = x.shape[0]
            return res[:n] + res[n:]

        def send(stage, d, to):
            copy = pltpu.make_async_remote_copy(
                src_ref=sbuf.at[stage, d], dst_ref=rbuf.at[stage, d],
                send_sem=s_sem.at[stage, d], recv_sem=r_sem.at[stage, d],
                device_id=(w, to), device_id_type=MESH,
            )
            copy.start()
            return copy

        pending = []

        def send_strips(stage, east, north, mat, offs):
            res = permute(jnp.concatenate([east, north], axis=1), mat)
            copies = []
            for d in range(2):
                sbuf[stage, d] = res[:, d * 256 : (d + 1) * 256]
            for d in range(2):
                copies.append(send(stage, d, fwd(offs[d])))
            pending.extend(copies)
            return copies

        def received(copies, stage):
            for copy in copies:
                copy.wait_recv()
            return rbuf[stage, 0] + rbuf[stage, 1]

        def roll2(x, shift):
            return jnp.concatenate([roll(x[:, :LANES], shift), roll(x[:, LANES:], shift)], axis=1)

        slot8 = jnp.where((l64_8 & 3) < 3, l64_8 >> 2, -1)

        def put(acc, x, v, first):
            return jnp.where(slot8 == v % 16, roll(x, 4 * (v % 16) - first), acc)

        def tile_rows(i):
            if isinstance(i, int):
                return pl.ds(8 * i, 8)
            return pl.ds(pl.multiple_of(8 * i, 8), 8)

        def pack_group(src, g, first, pad, us, start):
            acc = start
            for u in us:
                moved = roll(src[:, chunk(16 * g + u + pad)], 4 * u - first)
                acc = jnp.where(((l64 >> 2) == u) & ((l64 & 3) < 3), moved, acc)
            return acc

        def pack(dst, src, first, pad):
            for g in range(2):
                dst[:, pl.ds(g * LANES, LANES)] = pack_group(src, g, first, pad, range(16), jnp.zeros((rows, LANES), F32))

        build(wx, 0, off_x, 0, False)
        if levels < rows:
            qi[pl.ds(levels * NV, (rows - levels) * NV), :] = jnp.zeros(((rows - levels) * NV, LANES), F32)
        for i in range(tiles_of):
            fields[i].wait()
            acc = [jnp.zeros((8, LANES), F32)] * 2
            for v in range(NV):
                here = qi[pl.ds(8 * NV * i + v, 8, stride=NV), :]
                q[tile_rows(i), chunk(v)] = here
                acc[v // 16] = put(acc[v // 16], here, v, 61)
            epack[tile_rows(i), pl.ds(0, LANES)] = acc[0]
            epack[tile_rows(i), pl.ds(LANES, LANES)] = acc[1]

        strips = permute(jnp.concatenate([epack[...], q[:, pl.ds(CELLS - 256, 256)]], axis=1), wx)
        for d in range(2):
            sbuf[0, d] = strips[:, d * 256 : (d + 1) * 256]
        pl.semaphore_wait(barrier, len(partners))
        first = [send(0, d, fwd(off_x[d])) for d in range(2)]
        pending.extend(first)

        loads[0].wait()
        loads[1].wait()
        for c, cb in ((cx, cxb), (cy, cyb)):
            c[pl.ds(levels, rows - levels), :] = jnp.zeros((rows - levels, CELLS), F32)

            @pl.loop(0, NV // 8)
            def _(v, c=c, cb=cb):
                some = pl.ds(pl.multiple_of(v * 8 * LANES, 8 * LANES), 8 * LANES)
                c[pl.ds(0, levels), some] = cb[:, some].astype(F32)

        def x_interior():
            @pl.loop(0, tiles_of)
            def _(i):
                here_rows = tile_rows(i)
                ewrap[here_rows, :] = roll2(epack[here_rows, :], SIDE)
                acc = [jnp.zeros((8, LANES), F32)] * 2
                for v in range(NV):
                    here = q[here_rows, chunk(v)]
                    a1, a2, a3 = coefs(cx[here_rows, chunk(v)])
                    r1, r2, r3 = roll(here, 1), roll(here, 2), roll(here, 3)
                    flux = r1 * a1 + r2 * a2 + r3 * a3
                    outlet = here * a1 + r1 * a2 + r2 * a3
                    res = here + flux - jnp.where(l64_8 == SIDE - 1, outlet, roll(flux, -1))
                    bx[here_rows, chunk(v + 2)] = res
                    acc[v // 16] = put(acc[v // 16], res, v, 61)
                epack[here_rows, pl.ds(0, LANES)] = acc[0]
                epack[here_rows, pl.ds(LANES, LANES)] = acc[1]

        x_interior()

        for i in range(3):
            loads[4 + i].wait()
            x = sq[i]
            sq2[i, :, pl.ds(0, SIDE)] = x

        for i in range(3):
            x = sq2[i]
            sq2[i] = jnp.where(lanes_of((SIDE, LANES)) < SIDE, x, pltpu.roll(x, SIDE, 1))

        for i in range(3):
            @pl.loop(0, NV // 8)
            def _(k, i=i):
                for j in range(8):
                    v = k * 8 + j
                    row = jnp.where(low1, sq2[i, pl.ds(2 * v, 1), :], sq2[i, pl.ds(2 * v + 1, 1), :])
                    flat[i, :, chunk(v)] = jnp.broadcast_to(row, (8, LANES))

        loads[2].wait()
        loads[3].wait()
        diag = lax.broadcasted_iota(I32, (levels, levels), 0) == lax.broadcasted_iota(I32, (levels, levels), 1)
        for i, col in ((0, kcol), (1, pcol)):
            column = jnp.sum(jnp.where(diag, jnp.broadcast_to(kp[i], (levels, levels)), 0.0), axis=1, keepdims=True)
            col[...] = jnp.zeros((rows, LANES), F32)
            col[pl.ds(0, levels), :] = jnp.broadcast_to(column, (levels, LANES))
        inv = 1.0 / jnp.sum(kp[0], axis=1, keepdims=True)
        inv8 = jnp.broadcast_to(inv, (8, LANES))

        sset[pl.ds(0, rows), :] = cy[:, pl.ds(0, 256)]
        for i in range(2):
            sset[pl.ds(rows + 8 * i, 8), :] = flat[1 + i, :, pl.ds(0, 256)]
        sets = []
        for d in range(2):
            copy = pltpu.make_async_remote_copy(
                src_ref=sset, dst_ref=rset.at[d], send_sem=sset_sem.at[d], recv_sem=rset_sem.at[d],
                device_id=(w, bwd(off_y[d])), device_id_type=MESH,
            )
            copy.start()
            sets.append(copy)

        build(wy, 3, off_y, 1, False)

        pack(cpack, cx, 0, 0)
        part = lanes_of((rows, 256)) & 3
        p1, p2, p3 = coefs(cpack[...])
        west1 = jnp.where(part == 0, p1, 0.0)
        west2 = jnp.where(part <= 1, p2, 0.0)
        west3 = jnp.where(part <= 2, p3, 0.0)
        cpack3 = (west1, west2, west3)

        def west_change(panel):
            panel = panel - ewrap[...]
            f = panel * cpack3[2] + roll2(panel, -1) * cpack3[1] + roll2(panel, -2) * cpack3[0]
            return jnp.where(part < 3, f - roll2(f, -1), 0.0)

        def y_flux(qv_r, q1, q1_r, q2_r, c):
            a1, a2, a3 = coefs(c)
            s1 = jnp.where(low, q1_r, qv_r)
            return s1 * a1 + q1 * a2 + jnp.where(low, q2_r, q1_r) * a3

        def y_interior(here_rows, finish, fixed=0):
            changes = [dbuf[here_rows, pl.ds(g * LANES, LANES)] for g in range(2)]
            xs, rs, turned, outlet = {}, {}, {}, None
            done = {}
            for v in range(NV):
                xs[v] = bx[here_rows, chunk(v + 2)]
                if v >= fixed:
                    xs[v] = xs[v] + jnp.where(l64_8 < 3, roll(changes[v // 16], -4 * (v % 16)), 0.0)
                if fixed <= v < 3:
                    bx[here_rows, chunk(v + 2)] = xs[v]
                rs[v] = roll(xs[v], SIDE)
                if v < 2:
                    continue
                a1, a2, a3 = coefs(cy[here_rows, chunk(v)])
                flux = jnp.where(low8, rs[v - 1], rs[v]) * a1 + xs[v - 1] * a2 + jnp.where(low8, rs[v - 2], rs[v - 1]) * a3
                turned[v] = roll(flux, SIDE)
                done[v] = xs[v] + flux
                if v > 2:
                    finish(v - 1, done[v - 1] - jnp.where(low8, turned[v - 1], turned[v]))
                if v == NV - 1:
                    outlet = xs[v] * a1 + jnp.where(low8, rs[v - 1], rs[v]) * a2 + xs[v - 1] * a3
                    finish(v, done[v] - jnp.where(low8, turned[v], outlet))

        def y_first(pa, pb):
            q0_, q1_, q2_ = bx[:, chunk(2)], bx[:, chunk(3)], bx[:, chunk(4)]
            t0, t1, t2 = roll(q0_, SIDE), roll(q1_, SIDE), roll(q2_, SIDE)
            ta, tb = roll(pa, SIDE), roll(pb, SIDE)
            above = roll(y_flux(t2, q1_, t1, t0, cy[:, chunk(2)]), SIDE)
            f1 = y_flux(t1, q0_, t0, tb, cy[:, chunk(1)])
            f0 = y_flux(t0, pb, tb, ta, cy[:, chunk(0)])
            g1, g0 = roll(f1, SIDE), roll(f0, SIDE)
            n1 = q1_ + f1 - jnp.where(low, g1, above) + emitted(1)
            n0 = q0_ + f0 - jnp.where(low, g0, g1) + emitted(0)
            return n0, n1

        def emitted(v):
            return pcol[...] * jnp.concatenate([flat[0, :, chunk(v)]] * (rows // 8), axis=0)

        def sum_levels(x):
            acc = x[0:8]
            for i in range(1, rows // 8):
                acc = acc + x[8 * i : 8 * i + 8]
            return acc

        def down(x):
            return jnp.broadcast_to(jnp.sum(x, axis=0, keepdims=True), (8, LANES))

        def tall(x):
            return jnp.concatenate([x] * (rows // 8), axis=0)

        panel = received(first, 0)
        dbuf[...] = west_change(panel)
        change = dbuf[:, pl.ds(LANES, LANES)]
        ends_now = [
            bx[:, chunk(v + 2)] + jnp.where(l64 < 3, roll(change, -4 * (v % 16)), 0.0) for v in (NV - 2, NV - 1)
        ]
        y1 = send_strips(1, epack[...], jnp.concatenate(ends_now, axis=1), wy, off_y)

        @pl.loop(0, tiles_of)
        def _(i):
            here_rows = tile_rows(i)
            acc = [jnp.zeros((8, LANES), F32)] * 2
            share = pcol[here_rows, :]

            def finish(v, res):
                res = res + share * flat[0, :, chunk(v)]
                q[here_rows, chunk(v)] = res
                acc[v // 16] = put(acc[v // 16], res, v, 61)

            y_interior(here_rows, finish)
            epack[here_rows, pl.ds(0, LANES)] = acc[0]
            epack[here_rows, pl.ds(LANES, LANES)] = acc[1]

        panel = received(y1, 1)
        for v, res in enumerate(y_first(panel[:, :LANES], panel[:, LANES:])):
            q[:, chunk(v)] = res
        epack[:, pl.ds(0, LANES)] = pack_group(q, 0, 61, 0, range(2), epack[:, pl.ds(0, LANES)])

        x2 = send_strips(2, epack[...], q[:, pl.ds(CELLS - 256, 256)], wx, off_x)
        x_interior()
        build(wyt, 3, off_y, 1, True)
        for copy in sets:
            copy.wait_recv()

        panel = received(x2, 2)
        dbuf[...] = west_change(panel)
        change = dbuf[:, pl.ds(LANES, LANES)]
        ends_now = [
            bx[:, chunk(v + 2)] + jnp.where(l64 < 3, roll(change, -4 * (v % 16)), 0.0) for v in (NV - 2, NV - 1)
        ]
        y2 = send_strips(3, epack[...], jnp.concatenate(ends_now, axis=1), wy, off_y)

        def misfit_weight(col, v_obs, v_pre):
            return v_pre * (col * inv8 - v_obs) * inv8

        k_all = kcol[...]
        zero = jnp.zeros((rows, LANES), F32)
        change = dbuf[:, pl.ds(0, LANES)]
        for v in range(3):
            bx[:, chunk(v + 2)] = bx[:, chunk(v + 2)] + jnp.where(l64 < 3, roll(change, -4 * v), 0.0)
        for v, n in enumerate(y_first(zero, zero)):
            scol[:, chunk(v)] = down(sum_levels(n * k_all))
        cols = []
        for d in range(2):
            copy = pltpu.make_async_remote_copy(
                src_ref=scol, dst_ref=rcol.at[d], send_sem=scol_sem.at[d], recv_sem=rcol_sem.at[d],
                device_id=(w, bwd(off_y[d])), device_id_type=MESH,
            )
            copy.start()
            cols.append(copy)

        gf[...] = jnp.zeros((8, CELLS), F32)

        @pl.loop(0, tiles_of)
        def _(i):
            here_rows = tile_rows(i)
            share, weight = pcol[here_rows, :], kcol[here_rows, :]

            def finish(v, res):
                gf[:, chunk(v)] = gf[:, chunk(v)] + (res + share * flat[0, :, chunk(v)]) * weight

            y_interior(here_rows, finish, 3)

        def weigh(v, col):
            gf[:, chunk(v)] = misfit_weight(col, flat[1, :, chunk(v)], flat[2, :, chunk(v)])

        def slope(v):
            here = gf[:, chunk(v)]
            before = roll(gf[:, chunk(v - 1)], SIDE) if v > 0 else jnp.zeros((8, LANES), F32)
            return here - jnp.where(low8, before, roll(here, SIDE))

        for v in range(2, NV):
            weigh(v, down(gf[:, chunk(v)]))
        for v in range(2, NV):
            df[:, chunk(v)] = slope(v)

        @pl.loop(0, tiles_of)
        def _(i):
            here_rows = tile_rows(i)
            weight = kcol[here_rows, :]
            none = jnp.zeros((8, LANES), F32)
            top = -weight * roll(gf[:, chunk(NV - 1)], SIDE)
            b1, b2, b3 = coefs(roll(cy[here_rows, chunk(NV - 1)], SIDE))
            first_up = roll(jnp.where(low8, top * b1, 0.0), SIDE)
            second_up = jnp.where(low8, top * b2, 0.0)
            third_up, third_up2 = roll(jnp.where(low8, top * b3, 0.0), SIDE), none
            acc = [none, none]
            for v in range(NV - 1, 1, -1):
                bar = weight * df[:, chunk(v)]
                a1, a2, a3 = coefs(cy[here_rows, chunk(v)])
                turned1, turned3 = roll(bar * a1, SIDE), roll(bar * a3, SIDE)
                res = (
                    weight * gf[:, chunk(v)]
                    + jnp.where(low8, turned1, first_up)
                    + second_up
                    + jnp.where(low8, third_up, third_up2)
                )
                mu[here_rows, chunk(v)] = res
                if v < NV - 2:
                    acc[v // 16] = put(acc[v // 16], res, v, 0)
                first_up, second_up, third_up, third_up2 = turned1, bar * a2, turned3, third_up
            dbuf[here_rows, pl.ds(0, LANES)] = acc[0]
            dbuf[here_rows, pl.ds(LANES, LANES)] = acc[1]

        build(wxt, 0, off_x, 0, True)

        bars = []
        for d in range(2):
            cols[d].wait_recv()
            pa, pb = sbuf[3, d, :, pl.ds(0, LANES)], sbuf[3, d, :, pl.ds(LANES, LANES)]
            ra, rb = roll(pa, SIDE), roll(pb, SIDE)
            c0, c1 = rset[d, pl.ds(0, rows), pl.ds(0, LANES)], rset[d, pl.ds(0, rows), pl.ds(LANES, LANES)]
            z1, z2, z3 = coefs(c0)
            o1, o2, o3 = coefs(c1)
            h0 = jnp.where(low, rb, 0.0) * z1 + pb * z2 + jnp.where(low, ra, rb) * z3
            h1 = jnp.where(low, rb, 0.0) * o3
            k0, k1 = roll(h0, SIDE), roll(h1, SIDE)
            d0 = h0 - jnp.where(low, k0, k1)
            d1 = h1 - jnp.where(low, k1, 0.0)
            w0 = misfit_weight(
                rcol[d, :, chunk(0)] + down(sum_levels(d0 * k_all)),
                rset[d, pl.ds(rows, 8), chunk(0)], rset[d, pl.ds(rows + 8, 8), chunk(0)],
            )
            w1 = misfit_weight(
                rcol[d, :, chunk(1)] + down(sum_levels(d1 * k_all)),
                rset[d, pl.ds(rows, 8), chunk(1)], rset[d, pl.ds(rows + 8, 8), chunk(1)],
            )
            turned = roll(w0, SIDE)
            bar0 = k_all * tall(w0 - jnp.where(low8, 0.0, turned))
            bar1 = k_all * tall(w1 - jnp.where(low8, turned, roll(w1, SIDE)))
            third0, third1 = roll(bar0 * z3, SIDE), roll(bar1 * o3, SIDE)
            near_rows = jnp.where(low, 0.0, roll(bar0 * z1, SIDE)) + bar0 * z2 + jnp.where(low, third0, third1)
            far_rows = jnp.where(low, 0.0, third0)
            bars.append(jnp.concatenate([far_rows, near_rows], axis=1))
        back = permute(jnp.concatenate(bars, axis=1), wyt)
        back_east, back_north = back[:, :256], back[:, 256:]

        panel = received(y2, 3)
        for v, n in enumerate(y_first(panel[:, :LANES], panel[:, LANES:])):
            weigh(v, down(sum_levels(n * k_all)))
        made = {}
        for v in range(4):
            bar = k_all * tall(slope(v))
            a1, a2, a3 = coefs(cy[:, chunk(v)])
            made[v] = (roll(bar * a1, SIDE), bar * a2, roll(bar * a3, SIDE))
        for v in range(2):
            mu[:, chunk(v)] = (
                k_all * tall(gf[:, chunk(v)])
                + jnp.where(low, made[v][0], made[v + 1][0])
                + made[v + 1][1]
                + jnp.where(low, made[v + 1][2], made[v + 2][2])
            )
        mu[:, pl.ds(CELLS - 256, 256)] = mu[:, pl.ds(CELLS - 256, 256)] + back_north
        west0 = pack_group(mu, 0, 0, 0, range(2), dbuf[:, pl.ds(0, LANES)])
        west1_ = pack_group(mu, 1, 0, 0, range(14, 16), dbuf[:, pl.ds(LANES, LANES)])
        west = jnp.concatenate([west0, west1_], axis=1)
        diff = west - jnp.where(part > 0, roll2(west, 1), 0.0)
        pbar = diff * cpack3[2] + roll2(diff * cpack3[1], 1) + roll2(diff * cpack3[0], 2)
        p_all = pcol[...]
        for v in range(2):
            spb[:, chunk(v)] = down(sum_levels(pbar[:, v * LANES : (v + 1) * LANES] * p_all))
        finals = []
        for r in range(windows):
            for d in range(2):
                copy = pltpu.make_async_remote_copy(
                    src_ref=spb, dst_ref=rpb.at[d, r], send_sem=spb_sem.at[d, r], recv_sem=rpb_sem.at[d, r],
                    device_id=(win_of(r), bwd(off_x[d])), device_id_type=MESH,
                )
                copy.start()
                finals.append(copy)

        bfix[...] = back_east
        both = jnp.broadcast_to(jnp.sum(kcol[...] * pcol[...], axis=0, keepdims=True), (8, LANES))
        for v in range(NV):
            whole = mu[:, chunk(v)] + jnp.where(l64 >= 61, roll(bfix[:, pl.ds(v // 16 * LANES, LANES)], 61 - 4 * (v % 16)), 0.0)
            m = whole * p_all
            a1, a2, a3 = coefs(cx[:, chunk(v)])
            f = m - jnp.where(l64 >= 1, roll(m, 1), 0.0)
            s0 = sum_levels(m)
            s1, s2, s3 = sum_levels(f * a1), sum_levels(f * a2), sum_levels(f * a3)
            z1, z2, z3 = sum_levels(m * a1), sum_levels(m * a2), sum_levels(m * a3)
            res = s0 + jnp.where(l64_8 < 63, roll(s1, -1), -z1)
            res = res + jnp.where(l64_8 < 62, roll(s2, -2), jnp.where(l64_8 == 62, -roll(z2, -1), 0.0))
            res = res + jnp.where(l64_8 < 61, roll(s3, -3), jnp.where(l64_8 == 61, -roll(z3, -2), 0.0))
            gint[pl.ds(v, 1), :] = (down(res) + both * gf[:, chunk(v)])[0:1]

        sums = []
        for r in range(1, windows):
            to = win_of(r)
            copy = pltpu.make_async_remote_copy(
                src_ref=gint.at[pl.ds(pl.multiple_of(to * per, per), per), :], dst_ref=rg.at[r - 1],
                send_sem=sg_sem.at[r - 1], recv_sem=rg_sem.at[r - 1],
                device_id=(to, t), device_id_type=MESH,
            )
            copy.start()
            sums.append(copy)

        for copy in finals:
            copy.wait_recv()
        halves = []
        for d in range(2):
            acc = rpb[d, 0]
            for r in range(1, windows):
                acc = acc + rpb[d, r]
            halves.append(acc)
        ends = permute(jnp.concatenate(halves, axis=1), wxt)
        for v in range(NV):
            g, u = v // 16, v % 16
            row = jnp.where(l64_8 >= 61, roll(ends[:, g * LANES : (g + 1) * LANES], 61 - 4 * u), 0.0)
            if v >= NV - 2:
                at = 256 + (v - NV + 2) * LANES
                row = row + ends[:, at : at + LANES]
            fin[pl.ds(v, 1), :] = row[0:1]
        mine = pl.ds(pl.multiple_of(w * per, per), per)
        total = gint[mine, :] + fin[mine, :]
        for copy in sums:
            copy.wait_recv()
        for r in range(1, windows):
            total = total + rg[r - 1]
        out[0, pl.ds(0, per, stride=2), :] = total[:, :SIDE]
        out[0, pl.ds(1, per, stride=2), :] = pltpu.roll(total, SIDE, 1)[:, :SIDE]

        for copy in pending + sets + cols + finals + sums:
            copy.wait_send()

    return kernel, rows, per


def body(initial, courant_x, courant_y, observed, precision_w, kernel, profile, emission, edges):
    levels = initial.shape[2]
    windows = lax.axis_size("win")
    run, rows, per = make_kernel(levels, windows)
    vm = pltpu.VMEM
    dma = pltpu.SemaphoreType.DMA
    anywhere = pl.BlockSpec(memory_space=pl.ANY)
    return pl.pallas_call(
        run,
        out_shape=jax.ShapeDtypeStruct((1, 2 * per, SIDE), F32),
        in_specs=[anywhere] * 8 + [pl.BlockSpec(memory_space=pltpu.SMEM)],
        out_specs=pl.BlockSpec(memory_space=pltpu.VMEM),
        scratch_shapes=[
            vm((rows * NV, LANES), F32),
            vm((rows, CELLS), F32),
            vm((rows, CELLS + 256), F32),
            vm((rows, CELLS), F32),
            vm((rows, CELLS), F32),
            vm((rows, CELLS), F32),
            vm((levels, CELLS), BF16),
            vm((levels, CELLS), BF16),
            vm((3, SIDE, SIDE), F32),
            vm((3, SIDE, LANES), F32),
            vm((3, 8, CELLS), F32),
            vm((2, 1, levels), F32),
            vm((rows, LANES), F32),
            vm((rows, LANES), F32),
            vm((8, CELLS), F32),
            vm((8, CELLS), F32),
            vm((rows, 256), F32),
            vm((512, 512), BF16),
            vm((512, 512), BF16),
            vm((512, 512), BF16),
            vm((512, 512), BF16),
            vm((rows, 256), F32),
            vm((rows, 256), F32),
            vm((rows, 256), F32),
            vm((rows, 256), F32),
            vm((4, 2, rows, 256), F32),
            vm((4, 2, rows, 256), F32),
            vm((rows + 16, 256), F32),
            vm((2, rows + 16, 256), F32),
            vm((8, 256), F32),
            vm((2, 8, 256), F32),
            vm((8, 256), F32),
            vm((2, windows, 8, 256), F32),
            vm((NV, LANES), F32),
            vm((windows - 1, per, LANES), F32),
            vm((NV, LANES), F32),
            dma((7 + rows // 8,)),
            dma((4, 2)),
            dma((4, 2)),
            dma((2,)),
            dma((2,)),
            dma((2,)),
            dma((2,)),
            dma((2, windows)),
            dma((2, windows)),
            dma((windows - 1,)),
            dma((windows - 1,)),
        ],
        compiler_params=pltpu.CompilerParams(collective_id=0, has_side_effects=True),
    )(
        initial.reshape(levels * NV, LANES), courant_x, courant_y, observed, precision_w,
        kernel.reshape(1, levels), profile.reshape(1, levels), emission, edges,
    )


def solution(mesh):
    placed = (
        P("win", "tile", None, None),
        P("win", "tile", None, None),
        P("win", "tile", None, None),
        P("win", "tile", None, None),
        P("win", "tile", None, None),
        P(),
        P(),
        P("tile", None, None),
        P(),
    )
    return jax.shard_map(
        body, mesh=mesh, in_specs=placed, out_specs=P("tile", "win", None), check_vma=False
    )
```

```python
import jax
import jax.numpy as jnp
from jax import lax
from jax.experimental import pallas as pl
from jax.experimental.pallas import tpu as pltpu
from jax.sharding import PartitionSpec as P

F32 = jnp.float32
BF16 = jnp.bfloat16
I32 = jnp.int32
SIDE = 64
LANES = 128
CELLS = SIDE * SIDE
NV = CELLS // LANES
MESH = pl.DeviceIdType.MESH


def roll(x, shift):
    return pltpu.roll(x, shift % LANES, 1)


def lanes_of(shape):
    return lax.broadcasted_iota(I32, shape, 1)


def coefs(c):
    one, three = jnp.minimum(c, 1.0), jnp.maximum(c - 2.0, 0.0)
    return one, c - one - three, three


def chunk(v):
    if isinstance(v, int):
        return pl.ds(v * LANES, LANES)
    return pl.ds(pl.multiple_of(v * LANES, LANES), LANES)


def slot_key(index):
    part = index & 3
    cell = 32 * (index >> 7) + 2 * ((index >> 2) & 15) + ((index >> 6) & 1)
    return part * SIDE + cell, part < 3


def north_key(index):
    return index - SIDE, index >= SIDE


def make_kernel(levels, windows):
    rows = (levels + 7) // 8 * 8
    per = NV // windows

    def kernel(
        init_h, cx_h, cy_h, obs_h, pre_h, ker_h, pro_h, emi_h, edges,
        out,
        qi, q, bx, mu, cx, cy, cxb, cyb, sq, sq2, flat, kp, kcol, pcol, gf, df, bfix,
        wx, wxt, wy, wyt, epack, ewrap, cyp, cpack, dbuf,
        sbuf, rbuf, sy, ry, sdc, rdc, sset, rset, scol, rcol, spb, rpb, gint, rg, fin,
        in_sem, s_sem, r_sem, sset_sem, rset_sem, scol_sem, rcol_sem, spb_sem, rpb_sem, sg_sem, rg_sem, near_sem,
    ):
        w = lax.axis_index("win")
        t = lax.axis_index("tile")
        tiles = lax.axis_size("tile")
        off_x = (1, tiles // 4)
        off_y = (2, tiles // 2)

        def fwd(off):
            return lax.rem(t + off, tiles)

        def bwd(off):
            return lax.rem(t + tiles - off, tiles)

        def win_of(r):
            return lax.rem(w + r, windows)

        loads = [
            pltpu.make_async_copy(cx_h.at[0, 0], cxb, in_sem.at[0]),
            pltpu.make_async_copy(cy_h.at[0, 0], cyb, in_sem.at[1]),
            pltpu.make_async_copy(ker_h, kp.at[0], in_sem.at[2]),
            pltpu.make_async_copy(pro_h, kp.at[1], in_sem.at[3]),
            pltpu.make_async_copy(emi_h.at[0], sq.at[0], in_sem.at[4]),
            pltpu.make_async_copy(obs_h.at[0, 0], sq.at[1], in_sem.at[5]),
            pltpu.make_async_copy(pre_h.at[0, 0], sq.at[2], in_sem.at[6]),
        ]
        tiles_of = rows // 8
        fields = []
        for i in range(tiles_of):
            some = pl.ds(8 * NV * i, NV * min(8, levels - 8 * i))
            fields.append(pltpu.make_async_copy(init_h.at[some, :], qi.at[some, :], in_sem.at[7 + i]))
        for load in fields + loads:
            load.start()

        barrier = pltpu.get_barrier_semaphore()
        partners = [(w, fwd(off)) for off in (1, tiles // 4, tiles - tiles // 4, tiles - 1)]
        partners += [(win_of(r), t) for r in range(1, windows)]
        for who in partners:
            pl.semaphore_signal(barrier, inc=1, device_id=who, device_id_type=MESH)

        lane = lanes_of((rows, LANES))
        l64 = lane & (SIDE - 1)
        low = lane < SIDE
        lane8 = lanes_of((8, LANES))
        l64_8 = lane8 & (SIDE - 1)
        low8 = lane8 < SIDE
        lane1 = lanes_of((1, LANES))
        low1 = lane1 < SIDE

        row_index = lax.broadcasted_iota(I32, (256, LANES), 0)

        def rows_key(kind):
            key, valid = (slot_key if kind == 0 else north_key)(row_index)
            return jnp.where(valid, key, -1000)

        def cols_key(kind, half):
            key, valid = (slot_key if kind == 0 else north_key)(lane1 + half * LANES)
            return jnp.where(valid, key, -2000)

        def choices(base, offs):
            out_ = []
            for off in offs:
                to = fwd(off)
                mine = (edges[base, to] == t).astype(I32)
                code = edges[base + 1, to]
                flip = edges[base + 2, to]
                out_.append((63 * flip, 4096 * (1 - mine * (1 - code)), 4096 * (1 - mine * code)))
            return out_

        row_keys = (rows_key(0), rows_key(1))

        def hot(mask):
            return jnp.where(mask, 1.0, 0.0).astype(BF16)

        def build(mat, base, offs, kind, transposed):
            for d, (flip, not_east, not_north) in enumerate(choices(base, offs)):
                for src in range(2):
                    away = not_east if src == 0 else not_north
                    for half in range(2):
                        if transposed:
                            cols = (cols_key(src, half) ^ flip) + away
                            mat[pl.ds(d * 256, 256), pl.ds(src * 256 + half * LANES, LANES)] = hot(row_keys[kind] == cols)
                        else:
                            cols = (cols_key(kind, half) ^ flip) + away
                            mat[pl.ds(src * 256, 256), pl.ds(d * 256 + half * LANES, LANES)] = hot(row_keys[src] == cols)

        def permute(x, mat):
            top = x.astype(BF16).astype(F32)
            both = jnp.concatenate([top, x - top], axis=0).astype(BF16)
            res = jnp.dot(both, mat[...], preferred_element_type=F32)
            n = x.shape[0]
            return res[:n] + res[n:]

        def send(stage, d, to):
            copy = pltpu.make_async_remote_copy(
                src_ref=sbuf.at[stage, d], dst_ref=rbuf.at[stage, d],
                send_sem=s_sem.at[stage, d], recv_sem=r_sem.at[stage, d],
                device_id=(w, to), device_id_type=MESH,
            )
            copy.start()
            return copy

        pending = []

        def send_strips(stage, east, north, mat, offs):
            res = permute(jnp.concatenate([east, north], axis=1), mat)
            copies = []
            for d in range(2):
                sbuf[stage, d] = res[:, d * 256 : (d + 1) * 256]
            for d in range(2):
                copies.append(send(stage, d, fwd(offs[d])))
            pending.extend(copies)
            return copies

        pairs, odd = tiles_of // 2, tiles_of % 2
        fold = odd == 1 and 0 < levels % 8 <= 4
        packed = 8 * (tiles_of + pairs + (odd == 1 and not fold))
        sub8 = lax.broadcasted_iota(I32, (8, LANES), 0)

        def squeeze(x):
            far, near_two = x[:, :LANES], x[:, LANES:]
            pieces = [near_two[8 * i : 8 * i + 8] for i in range(tiles_of)]
            extra = [
                jnp.where(low8, roll(far[16 * i : 16 * i + 8], SIDE), far[16 * i + 8 : 16 * i + 16]) for i in range(pairs)
            ]
            if odd:
                tail = roll(far[rows - 8 :], SIDE)
                if fold:
                    pieces[-1] = jnp.where(sub8 < 4, pieces[-1], pltpu.roll(tail, 4, 0))
                else:
                    extra.append(tail)
            return jnp.concatenate(pieces + extra, axis=0)

        def unsqueeze(x):
            near_two = [x[8 * i : 8 * i + 8] for i in range(tiles_of)]
            far = []
            for i in range(pairs):
                both_ = x[rows + 8 * i : rows + 8 * i + 8]
                far += [both_, roll(both_, SIDE)]
            if odd:
                if fold:
                    far.append(jnp.where(sub8 < 4, pltpu.roll(near_two[-1], 4, 0), 0.0))
                    near_two[-1] = jnp.where(sub8 < 4, near_two[-1], 0.0)
                else:
                    far.append(x[rows + 8 * pairs : rows + 8 * pairs + 8])
            return jnp.concatenate(near_two, axis=0), jnp.concatenate(far, axis=0)

        def received(copies, stage):
            for copy in copies:
                copy.wait_recv()
            return rbuf[stage, 0] + rbuf[stage, 1]

        def roll2(x, shift):
            return jnp.concatenate([roll(x[:, :LANES], shift), roll(x[:, LANES:], shift)], axis=1)

        slot8 = jnp.where((l64_8 & 3) < 3, l64_8 >> 2, -1)

        def put(acc, x, v, first):
            return jnp.where(slot8 == v % 16, roll(x, 4 * (v % 16) - first), acc)

        def tile_rows(i):
            if isinstance(i, int):
                return pl.ds(8 * i, 8)
            return pl.ds(pl.multiple_of(8 * i, 8), 8)

        def pack_group(src, g, first, pad, us, start):
            acc = start
            for u in us:
                moved = roll(src[:, chunk(16 * g + u + pad)], 4 * u - first)
                acc = jnp.where(((l64 >> 2) == u) & ((l64 & 3) < 3), moved, acc)
            return acc

        def pack(dst, src, first, pad):
            for g in range(2):
                dst[:, pl.ds(g * LANES, LANES)] = pack_group(src, g, first, pad, range(16), jnp.zeros((rows, LANES), F32))

        build(wx, 0, off_x, 0, False)
        if levels < rows:
            qi[pl.ds(levels * NV, (rows - levels) * NV), :] = jnp.zeros(((rows - levels) * NV, LANES), F32)
        for i in range(tiles_of):
            fields[i].wait()
            acc = [jnp.zeros((8, LANES), F32)] * 2
            for v in range(NV):
                here = qi[pl.ds(8 * NV * i + v, 8, stride=NV), :]
                q[tile_rows(i), chunk(v)] = here
                acc[v // 16] = put(acc[v // 16], here, v, 61)
            epack[tile_rows(i), pl.ds(0, LANES)] = acc[0]
            epack[tile_rows(i), pl.ds(LANES, LANES)] = acc[1]

        strips = permute(jnp.concatenate([epack[...], q[:, pl.ds(CELLS - 256, 256)]], axis=1), wx)
        for d in range(2):
            sbuf[0, d] = strips[:, d * 256 : (d + 1) * 256]
        pl.semaphore_wait(barrier, len(partners))
        first = [send(0, d, fwd(off_x[d])) for d in range(2)]
        for who in partners:
            pl.semaphore_signal(near_sem, inc=1, device_id=who, device_id_type=MESH)
        pending.extend(first)
        build(wy, 3, off_y, 1, False)

        def widen(c, cb):
            c[pl.ds(levels, rows - levels), :] = jnp.zeros((rows - levels, CELLS), F32)

            @pl.loop(0, NV // 8)
            def _(v):
                some = pl.ds(pl.multiple_of(v * 8 * LANES, 8 * LANES), 8 * LANES)
                c[pl.ds(0, levels), some] = cb[:, some].astype(F32)

        loads[0].wait()
        widen(cx, cxb)

        def x_interior():
            @pl.loop(0, tiles_of)
            def _(i):
                here_rows = tile_rows(i)
                ewrap[here_rows, :] = roll2(epack[here_rows, :], SIDE)
                acc = [jnp.zeros((8, LANES), F32)] * 2
                for v in range(NV):
                    here = q[here_rows, chunk(v)]
                    a1, a2, a3 = coefs(cx[here_rows, chunk(v)])
                    r1, r2, r3 = roll(here, 1), roll(here, 2), roll(here, 3)
                    flux = r1 * a1 + r2 * a2 + r3 * a3
                    outlet = here * a1 + r1 * a2 + r2 * a3
                    res = here + flux - jnp.where(l64_8 == SIDE - 1, outlet, roll(flux, -1))
                    bx[here_rows, chunk(v + 2)] = res
                    acc[v // 16] = put(acc[v // 16], res, v, 61)
                epack[here_rows, pl.ds(0, LANES)] = acc[0]
                epack[here_rows, pl.ds(LANES, LANES)] = acc[1]

        x_interior()

        pack(cpack, cx, 0, 0)
        part = lanes_of((rows, 256)) & 3
        p1, p2, p3 = coefs(cpack[...])
        west1 = jnp.where(part == 0, p1, 0.0)
        west2 = jnp.where(part <= 1, p2, 0.0)
        west3 = jnp.where(part <= 2, p3, 0.0)
        cpack3 = (west1, west2, west3)

        def west_change(panel):
            panel = panel - ewrap[...]
            f = panel * cpack3[2] + roll2(panel, -1) * cpack3[1] + roll2(panel, -2) * cpack3[0]
            return jnp.where(part < 3, f - roll2(f, -1), 0.0)

        def y_flux(qv_r, q1, q1_r, q2_r, c):
            a1, a2, a3 = coefs(c)
            s1 = jnp.where(low, q1_r, qv_r)
            return s1 * a1 + q1 * a2 + jnp.where(low, q2_r, q1_r) * a3

        def y_interior(here_rows, finish, changed):
            none = jnp.zeros((8, LANES), F32)
            xs, rs, turned, outlet = {-1: none, -2: none}, {-1: none, -2: none}, {}, None
            done = {}
            lowest = 2 if changed else 0
            for v in range(NV):
                xs[v] = bx[here_rows, chunk(v + 2)]
                if changed:
                    change = dbuf[here_rows, pl.ds(v // 16 * LANES, LANES)]
                    xs[v] = xs[v] + jnp.where(l64_8 < 3, roll(change, -4 * (v % 16)), 0.0)
                    if v < 3:
                        bx[here_rows, chunk(v + 2)] = xs[v]
                rs[v] = roll(xs[v], SIDE)
                if v < lowest:
                    continue
                a1, a2, a3 = coefs(cy[here_rows, chunk(v)])
                flux = jnp.where(low8, rs[v - 1], rs[v]) * a1 + xs[v - 1] * a2 + jnp.where(low8, rs[v - 2], rs[v - 1]) * a3
                turned[v] = roll(flux, SIDE)
                done[v] = xs[v] + flux
                if v > lowest:
                    finish(v - 1, done[v - 1] - jnp.where(low8, turned[v - 1], turned[v]))
                if v == NV - 1:
                    outlet = xs[v] * a1 + jnp.where(low8, rs[v - 1], rs[v]) * a2 + xs[v - 1] * a3
                    finish(v, done[v] - jnp.where(low8, turned[v], outlet))

        def y_first(ta, pb):
            q0_, q1_, q2_ = bx[:, chunk(2)], bx[:, chunk(3)], bx[:, chunk(4)]
            t0, t1, t2 = roll(q0_, SIDE), roll(q1_, SIDE), roll(q2_, SIDE)
            tb = roll(pb, SIDE)
            above = roll(y_flux(t2, q1_, t1, t0, cy[:, chunk(2)]), SIDE)
            f1 = y_flux(t1, q0_, t0, tb, cy[:, chunk(1)])
            f0 = y_flux(t0, pb, tb, ta, cy[:, chunk(0)])
            g1, g0 = roll(f1, SIDE), roll(f0, SIDE)
            n1 = q1_ + f1 - jnp.where(low, g1, above) + emitted(1)
            n0 = q0_ + f0 - jnp.where(low, g0, g1) + emitted(0)
            return n0, n1

        def emitted(v):
            return pcol[...] * jnp.concatenate([flat[0, :, chunk(v)]] * (rows // 8), axis=0)

        def sum_levels(x):
            acc = x[0:8]
            for i in range(1, rows // 8):
                acc = acc + x[8 * i : 8 * i + 8]
            return acc

        def down(x):
            return jnp.broadcast_to(jnp.sum(x, axis=0, keepdims=True), (8, LANES))

        def tall(x):
            return jnp.concatenate([x] * (rows // 8), axis=0)

        panel = received(first, 0)
        dbuf[...] = west_change(panel)
        change = dbuf[:, pl.ds(LANES, LANES)]
        ends_now = [
            bx[:, chunk(v + 2)] + jnp.where(l64 < 3, roll(change, -4 * (v % 16)), 0.0) for v in (NV - 2, NV - 1)
        ]
        res = permute(jnp.concatenate([epack[...]] + ends_now, axis=1), wy)
        for d in range(2):
            sy[d] = squeeze(res[:, d * 256 : (d + 1) * 256])
        pl.semaphore_wait(near_sem, len(partners))
        y1 = []
        for d in range(2):
            copy = pltpu.make_async_remote_copy(
                src_ref=sy.at[d], dst_ref=ry.at[d], send_sem=s_sem.at[1, d], recv_sem=r_sem.at[1, d],
                device_id=(w, fwd(off_y[d])), device_id_type=MESH,
            )
            copy.start()
            y1.append(copy)
        pending.extend(y1)

        loads[1].wait()
        widen(cy, cyb)
        for i in range(3):
            loads[4 + i].wait()
            x = sq[i]
            sq2[i, :, pl.ds(0, SIDE)] = x

        for i in range(3):
            x = sq2[i]
            sq2[i] = jnp.where(lanes_of((SIDE, LANES)) < SIDE, x, pltpu.roll(x, SIDE, 1))

        for i in range(3):
            @pl.loop(0, NV // 8)
            def _(k, i=i):
                for j in range(8):
                    v = k * 8 + j
                    row = jnp.where(low1, sq2[i, pl.ds(2 * v, 1), :], sq2[i, pl.ds(2 * v + 1, 1), :])
                    flat[i, :, chunk(v)] = jnp.broadcast_to(row, (8, LANES))

        loads[2].wait()
        loads[3].wait()
        diag = lax.broadcasted_iota(I32, (levels, levels), 0) == lax.broadcasted_iota(I32, (levels, levels), 1)
        for i, col in ((0, kcol), (1, pcol)):
            column = jnp.sum(jnp.where(diag, jnp.broadcast_to(kp[i], (levels, levels)), 0.0), axis=1, keepdims=True)
            col[...] = jnp.zeros((rows, LANES), F32)
            col[pl.ds(0, levels), :] = jnp.broadcast_to(column, (levels, LANES))
        inv = 1.0 / jnp.sum(kp[0], axis=1, keepdims=True)
        inv8 = jnp.broadcast_to(inv, (8, LANES))


        sset[pl.ds(0, packed), :] = squeeze(
            jnp.concatenate([roll(cy[:, chunk(1)], SIDE), cy[:, chunk(0)]], axis=1)
        )
        sset[pl.ds(packed + 4, 4), :] = jnp.zeros((4, LANES), F32)
        for i in range(2):
            for v in range(2):
                sset[pl.ds(packed + 2 * i + v, 1), :] = flat[1 + i, pl.ds(0, 1), chunk(v)]
        sets = []
        for d in range(2):
            copy = pltpu.make_async_remote_copy(
                src_ref=sset, dst_ref=rset.at[d], send_sem=sset_sem.at[d], recv_sem=rset_sem.at[d],
                device_id=(w, bwd(off_y[d])), device_id_type=MESH,
            )
            copy.start()
            sets.append(copy)

        @pl.loop(0, tiles_of)
        def _(i):
            here_rows = tile_rows(i)
            acc = [jnp.zeros((8, LANES), F32)] * 2
            share = pcol[here_rows, :]

            def finish(v, res):
                res = res + share * flat[0, :, chunk(v)]
                q[here_rows, chunk(v)] = res
                acc[v // 16] = put(acc[v // 16], res, v, 61)

            y_interior(here_rows, finish, True)
            epack[here_rows, pl.ds(0, LANES)] = acc[0]
            epack[here_rows, pl.ds(LANES, LANES)] = acc[1]

        build(wyt, 3, off_y, 1, True)
        build(wxt, 0, off_x, 0, True)
        pack(cyp, cy, 0, 0)
        for copy in y1:
            copy.wait_recv()
        near_two, far_one = unsqueeze(ry[0] + ry[1])
        east = epack[:, pl.ds(0, LANES)]
        for v, res in enumerate(y_first(far_one, near_two)):
            q[:, chunk(v)] = res
            east = jnp.where(((l64 >> 2) == v) & ((l64 & 3) < 3), roll(res, 4 * v - 61), east)
        epack[:, pl.ds(0, LANES)] = east

        x2 = send_strips(2, epack[...], q[:, pl.ds(CELLS - 256, 256)], wx, off_x)
        x_interior()
        for copy in sets:
            copy.wait_recv()

        gf[...] = jnp.zeros((8, CELLS), F32)

        @pl.loop(0, tiles_of)
        def _(i):
            here_rows = tile_rows(i)
            share, weight = pcol[here_rows, :], kcol[here_rows, :]

            def finish(v, res):
                gf[:, chunk(v)] = gf[:, chunk(v)] + (res + share * flat[0, :, chunk(v)]) * weight

            y_interior(here_rows, finish, False)

        def slots(x):
            index = lanes_of(x.shape)
            return (index >> 6) & 1, (index >> 2) & 15

        def shift_down(x):
            high, u = slots(x[0])
            res = []
            for g in range(2):
                over = roll(x[g - 1], 4) if g > 0 else jnp.zeros_like(x[0])
                res.append(jnp.where(high == 1, roll(x[g], SIDE), jnp.where(u == 0, over, roll(x[g], 68))))
            return res

        def shift_down2(x):
            u = slots(x[0])[1]
            res = []
            for g in range(2):
                over = roll(x[g - 1], 68) if g > 0 else jnp.zeros_like(x[0])
                res.append(jnp.where(u == 0, over, roll(x[g], 4)))
            return res

        def shift_up(x, after):
            high, u = slots(x[0])
            res = []
            for g in range(2):
                over = roll(x[g + 1], 124) if g == 0 else after
                res.append(jnp.where(high == 0, roll(x[g], SIDE), jnp.where(u == 15, over, roll(x[g], 60))))
            return res

        ca = [coefs(cyp[:, pl.ds(g * LANES, LANES)]) for g in range(2)]
        k_all = kcol[...]
        zero = jnp.zeros((rows, LANES), F32)

        panel = received(x2, 2)
        dbuf[...] = west_change(panel)
        change = dbuf[:, pl.ds(LANES, LANES)]
        ends_now = [
            bx[:, chunk(v + 2)] + jnp.where(l64 < 3, roll(change, -4 * (v % 16)), 0.0) for v in (NV - 2, NV - 1)
        ]
        panels = permute(jnp.concatenate([epack[...]] + ends_now, axis=1), wy)

        def misfit_weight(col, v_obs, v_pre):
            return v_pre * (col * inv8 - v_obs) * inv8

        new = [dbuf[:, pl.ds(g * LANES, LANES)] for g in range(2)]
        s1, s2 = shift_down(new), shift_down2(new)
        s3 = shift_down(s2)
        flow = [s1[g] * ca[g][0] + s2[g] * ca[g][1] + s3[g] * ca[g][2] for g in range(2)]
        out_flow = shift_up(flow, new[1] * ca[1][0] + s1[1] * ca[1][1] + s2[1] * ca[1][2])
        gained = [sum_levels((new[g] + flow[g] - out_flow[g]) * k_all) for g in range(2)]

        def column(v):
            return down(gf[:, chunk(v)] + jnp.where(l64_8 < 3, roll(gained[v // 16], -4 * (v % 16)), 0.0))

        for v in range(2):
            scol[:, chunk(v)] = column(v)[0:1]
        cols = []
        for d in range(2):
            copy = pltpu.make_async_remote_copy(
                src_ref=scol, dst_ref=rcol.at[d], send_sem=scol_sem.at[d], recv_sem=rcol_sem.at[d],
                device_id=(w, bwd(off_y[d])), device_id_type=MESH,
            )
            copy.start()
            cols.append(copy)

        effects, edge = [], []
        for d in range(2):
            pa, pb = panels[:, d * 256 : d * 256 + LANES], panels[:, d * 256 + LANES : d * 256 + 256]
            ra, rb = roll(pa, SIDE), roll(pb, SIDE)
            c0, c1 = unsqueeze(rset[d, pl.ds(0, packed), :])
            z1, z2, z3 = coefs(c0)
            o3 = coefs(c1)[2]
            edge.append((z1, z2, z3, o3))
            h0 = jnp.where(low, rb, 0.0) * z1 + pb * z2 + jnp.where(low, ra, rb) * z3
            h1 = jnp.where(low, rb, 0.0) * o3
            k0, k1 = roll(h0, SIDE), roll(h1, SIDE)
            d0 = h0 - jnp.where(low, k0, k1)
            d1 = h1 - jnp.where(low, k1, 0.0)
            effects.append((down(sum_levels(d0 * k_all)), down(sum_levels(d1 * k_all))))
            for v in range(2):
                sdc[d, :, chunk(v)] = effects[d][v][0:1]
        for d in range(2):
            copy = pltpu.make_async_remote_copy(
                src_ref=sdc.at[d], dst_ref=rdc.at[d], send_sem=s_sem.at[3, d], recv_sem=r_sem.at[3, d],
                device_id=(w, fwd(off_y[d])), device_id_type=MESH,
            )
            copy.start()
            pending.append(copy)

        def weigh(v, col):
            gf[:, chunk(v)] = misfit_weight(col, flat[1, :, chunk(v)], flat[2, :, chunk(v)])

        def slope(v):
            here = gf[:, chunk(v)]
            before = roll(gf[:, chunk(v - 1)], SIDE) if v > 0 else jnp.zeros((8, LANES), F32)
            return here - jnp.where(low8, before, roll(here, SIDE))

        for v in range(2, NV):
            weigh(v, column(v))
        gf[:, pl.ds(0, 256)] = jnp.zeros((8, 256), F32)
        for v in range(2, NV):
            df[:, chunk(v)] = slope(v)

        @pl.loop(0, tiles_of)
        def _(i):
            here_rows = tile_rows(i)
            weight = kcol[here_rows, :]
            none = jnp.zeros((8, LANES), F32)
            top = -weight * roll(gf[:, chunk(NV - 1)], SIDE)
            b1, b2, b3 = coefs(roll(cy[here_rows, chunk(NV - 1)], SIDE))
            first_up = roll(jnp.where(low8, top * b1, 0.0), SIDE)
            second_up = jnp.where(low8, top * b2, 0.0)
            third_up, third_up2 = roll(jnp.where(low8, top * b3, 0.0), SIDE), none
            acc = [none, none]
            for v in range(NV - 1, 1, -1):
                bar = weight * df[:, chunk(v)]
                a1, a2, a3 = coefs(cy[here_rows, chunk(v)])
                turned1, turned3 = roll(bar * a1, SIDE), roll(bar * a3, SIDE)
                res = (
                    weight * gf[:, chunk(v)]
                    + jnp.where(low8, turned1, first_up)
                    + second_up
                    + jnp.where(low8, third_up, third_up2)
                )
                mu[here_rows, chunk(v)] = res
                if v < NV - 2:
                    acc[v // 16] = put(acc[v // 16], res, v, 0)
                first_up, second_up, third_up, third_up2 = turned1, bar * a2, turned3, third_up
            dbuf[here_rows, pl.ds(0, LANES)] = acc[0]
            dbuf[here_rows, pl.ds(LANES, LANES)] = acc[1]

        bars = []
        for d in range(2):
            cols[d].wait_recv()
            z1, z2, z3, o3 = edge[d]
            w0, w1 = (
                misfit_weight(
                    jnp.broadcast_to(rcol[d, :, chunk(v)], (8, LANES)) + effects[d][v],
                    jnp.broadcast_to(rset[d, pl.ds(packed + v, 1), :], (8, LANES)),
                    jnp.broadcast_to(rset[d, pl.ds(packed + 2 + v, 1), :], (8, LANES)),
                )
                for v in range(2)
            )
            turned = roll(w0, SIDE)
            bar0 = k_all * tall(w0 - jnp.where(low8, 0.0, turned))
            bar1 = k_all * tall(w1 - jnp.where(low8, turned, roll(w1, SIDE)))
            third0, third1 = roll(bar0 * z3, SIDE), roll(bar1 * o3, SIDE)
            near_rows = jnp.where(low, 0.0, roll(bar0 * z1, SIDE)) + bar0 * z2 + jnp.where(low, third0, third1)
            far_rows = jnp.where(low, 0.0, third0)
            bars.append(jnp.concatenate([far_rows, near_rows], axis=1))
        back = permute(jnp.concatenate(bars, axis=1), wyt)
        back_east, back_north = back[:, :256], back[:, 256:]

        for copy in pending[-2:]:
            copy.wait_recv()
        for v in range(2):
            weigh(v, jnp.broadcast_to(scol[:, chunk(v)] + rdc[0, :, chunk(v)] + rdc[1, :, chunk(v)], (8, LANES)))
        made = {}
        for v in range(4):
            bar = k_all * tall(slope(v))
            a1, a2, a3 = coefs(cy[:, chunk(v)])
            made[v] = (roll(bar * a1, SIDE), bar * a2, roll(bar * a3, SIDE))
        for v in range(2):
            mu[:, chunk(v)] = (
                k_all * tall(gf[:, chunk(v)])
                + jnp.where(low, made[v][0], made[v + 1][0])
                + made[v + 1][1]
                + jnp.where(low, made[v + 1][2], made[v + 2][2])
            )
        mu[:, pl.ds(CELLS - 256, 256)] = mu[:, pl.ds(CELLS - 256, 256)] + back_north
        west0 = pack_group(mu, 0, 0, 0, range(2), dbuf[:, pl.ds(0, LANES)])
        west1_ = pack_group(mu, 1, 0, 0, range(14, 16), dbuf[:, pl.ds(LANES, LANES)])
        west = jnp.concatenate([west0, west1_], axis=1)
        diff = west - jnp.where(part > 0, roll2(west, 1), 0.0)
        pbar = diff * cpack3[2] + roll2(diff * cpack3[1], 1) + roll2(diff * cpack3[0], 2)
        p_all = pcol[...]
        for v in range(2):
            spb[:, chunk(v)] = down(sum_levels(pbar[:, v * LANES : (v + 1) * LANES] * p_all))[0:1]
        finals = []
        for r in range(windows):
            for d in range(2):
                copy = pltpu.make_async_remote_copy(
                    src_ref=spb, dst_ref=rpb.at[d, r], send_sem=spb_sem.at[d, r], recv_sem=rpb_sem.at[d, r],
                    device_id=(win_of(r), bwd(off_x[d])), device_id_type=MESH,
                )
                copy.start()
                finals.append(copy)

        bfix[...] = back_east
        both = jnp.broadcast_to(jnp.sum(kcol[...] * pcol[...], axis=0, keepdims=True), (8, LANES))
        sums = []
        for r in [*range(1, windows), 0]:
            to = win_of(r)
            side = lax.div(to * per, 16)
            east = bfix[:, chunk(side)]
            if per < 16:
                east = jnp.where(lax.rem(to * per, 16) == 8, roll(east, -32), east)
            for k in range(per):
                v = to * per + k
                whole = mu[:, chunk(v)] + jnp.where(l64 >= 61, roll(east, 61 - 4 * k), 0.0)
                m = whole * p_all
                c = cx[:, chunk(v)]
                a1, a2, a3 = coefs(jnp.where(l64 == 0, roll(c, 1), c))
                f = jnp.where(l64 == 0, 0.0, m) - roll(m, 1)
                s0 = sum_levels(m)
                s1, s2, s3 = sum_levels(f * a1), sum_levels(f * a2), sum_levels(f * a3)
                res = s0 + roll(s1, -1) + jnp.where(l64_8 < 63, roll(s2, -2), 0.0) + jnp.where(l64_8 < 62, roll(s3, -3), 0.0)
                gint[r, pl.ds(k, 1), :] = (down(res) + both * gf[:, chunk(v)])[0:1]
            if r > 0:
                copy = pltpu.make_async_remote_copy(
                    src_ref=gint.at[r], dst_ref=rg.at[r - 1],
                    send_sem=sg_sem.at[r - 1], recv_sem=rg_sem.at[r - 1],
                    device_id=(to, t), device_id_type=MESH,
                )
                copy.start()
                sums.append(copy)

        for copy in finals:
            copy.wait_recv()
        halves = []
        for d in range(2):
            acc = rpb[d, 0]
            for r in range(1, windows):
                acc = acc + rpb[d, r]
            halves.append(jnp.broadcast_to(acc, (8, 256)))
        ends = permute(jnp.concatenate(halves, axis=1), wxt)
        for v in range(NV):
            g, u = v // 16, v % 16
            row = jnp.where(l64_8 >= 61, roll(ends[:, g * LANES : (g + 1) * LANES], 61 - 4 * u), 0.0)
            if v >= NV - 2:
                at = 256 + (v - NV + 2) * LANES
                row = row + ends[:, at : at + LANES]
            fin[pl.ds(v, 1), :] = row[0:1]
        mine = pl.ds(pl.multiple_of(w * per, per), per)
        total = gint[0] + fin[mine, :]
        for copy in sums:
            copy.wait_recv()
        for r in range(1, windows):
            total = total + rg[r - 1]
        out[0, pl.ds(0, per, stride=2), :] = total[:, :SIDE]
        out[0, pl.ds(1, per, stride=2), :] = pltpu.roll(total, SIDE, 1)[:, :SIDE]

        for copy in pending + sets + cols + finals + sums:
            copy.wait_send()

    return kernel, rows, per


def body(initial, courant_x, courant_y, observed, precision_w, kernel, profile, emission, edges):
    levels = initial.shape[2]
    windows = lax.axis_size("win")
    run, rows, per = make_kernel(levels, windows)
    tiles_of = rows // 8
    packed = 8 * (tiles_of + tiles_of // 2 + (tiles_of % 2 == 1 and not 0 < levels % 8 <= 4))
    vm = pltpu.VMEM
    dma = pltpu.SemaphoreType.DMA
    anywhere = pl.BlockSpec(memory_space=pl.ANY)
    return pl.pallas_call(
        run,
        out_shape=pltpu.VMEM((1, 2 * per, SIDE), F32),
        in_specs=[anywhere] * 8 + [pl.BlockSpec(memory_space=pltpu.SMEM)],
        out_specs=pl.BlockSpec(memory_space=pltpu.VMEM),
        scratch_shapes=[
            vm((rows * NV, LANES), F32),
            vm((rows, CELLS), F32),
            vm((rows, CELLS + 256), F32),
            vm((rows, CELLS), F32),
            vm((rows, CELLS), F32),
            vm((rows, CELLS), F32),
            vm((levels, CELLS), BF16),
            vm((levels, CELLS), BF16),
            vm((3, SIDE, SIDE), F32),
            vm((3, SIDE, LANES), F32),
            vm((3, 8, CELLS), F32),
            vm((2, 1, levels), F32),
            vm((rows, LANES), F32),
            vm((rows, LANES), F32),
            vm((8, CELLS), F32),
            vm((8, CELLS), F32),
            vm((rows, 256), F32),
            vm((512, 512), BF16),
            vm((512, 512), BF16),
            vm((512, 512), BF16),
            vm((512, 512), BF16),
            vm((rows, 256), F32),
            vm((rows, 256), F32),
            vm((rows, 256), F32),
            vm((rows, 256), F32),
            vm((rows, 256), F32),
            vm((4, 2, rows, 256), F32),
            vm((4, 2, rows, 256), F32),
            vm((2, packed, LANES), F32),
            vm((2, packed, LANES), F32),
            vm((2, 1, 256), F32),
            vm((2, 1, 256), F32),
            vm((packed + 8, LANES), F32),
            vm((2, packed + 8, LANES), F32),
            vm((1, 256), F32),
            vm((2, 1, 256), F32),
            vm((1, 256), F32),
            vm((2, windows, 1, 256), F32),
            vm((windows, per, LANES), F32),
            vm((windows - 1, per, LANES), F32),
            vm((NV, LANES), F32),
            dma((7 + rows // 8,)),
            dma((4, 2)),
            dma((4, 2)),
            dma((2,)),
            dma((2,)),
            dma((2,)),
            dma((2,)),
            dma((2, windows)),
            dma((2, windows)),
            dma((windows - 1,)),
            dma((windows - 1,)),
            pltpu.SemaphoreType.REGULAR,
        ],
        compiler_params=pltpu.CompilerParams(collective_id=0, has_side_effects=True),
    )(
        initial.reshape(levels * NV, LANES), courant_x, courant_y, observed, precision_w,
        kernel.reshape(1, levels), profile.reshape(1, levels), emission, edges,
    )


def solution(mesh):
    placed = (
        P("win", "tile", None, None),
        P("win", "tile", None, None),
        P("win", "tile", None, None),
        P("win", "tile", None, None),
        P("win", "tile", None, None),
        P(),
        P(),
        P("tile", None, None),
        P(),
    )
    return jax.shard_map(
        body, mesh=mesh, in_specs=placed, out_specs=P("tile", "win", None), check_vma=False
    )
```

```python
import jax
import jax.numpy as jnp
from jax import lax
from jax.experimental import pallas as pl
from jax.experimental.pallas import tpu as pltpu
from jax.sharding import PartitionSpec as P

F32 = jnp.float32
BF16 = jnp.bfloat16
I32 = jnp.int32
SIDE = 64
LANES = 128
CELLS = SIDE * SIDE
NV = CELLS // LANES
MESH = pl.DeviceIdType.MESH


def roll(x, shift):
    return pltpu.roll(x, shift % LANES, 1)


def lanes_of(shape):
    return lax.broadcasted_iota(I32, shape, 1)


def coefs(c):
    one, three = jnp.minimum(c, 1.0), jnp.maximum(c - 2.0, 0.0)
    return one, c - one - three, three


def chunk(v):
    if isinstance(v, int):
        return pl.ds(v * LANES, LANES)
    return pl.ds(pl.multiple_of(v * LANES, LANES), LANES)


def slot_key(index):
    part = index & 3
    cell = 32 * (index >> 7) + 2 * ((index >> 2) & 15) + ((index >> 6) & 1)
    return part * SIDE + cell, part < 3


def north_key(index):
    return index - SIDE, index >= SIDE


def make_kernel(levels, windows):
    rows = (levels + 7) // 8 * 8
    per = NV // windows

    def kernel(
        init_h, cx_h, cy_h, obs_h, pre_h, ker_h, pro_h, emi_h, edges,
        out,
        qi, q, bx, mu, cx, cy, cxb, cyb, sq, sq2, flat, kp, kcol, pcol, gf, df, bfix,
        wx, wxt, wy, wyt, epack, ewrap, cyp, cpack, dbuf,
        sbuf, rbuf, sy, ry, sdc, rdc, sset, rset, scol, rcol, spb, rpb, gint, rg, fin,
        in_sem, s_sem, r_sem, sset_sem, rset_sem, scol_sem, rcol_sem, spb_sem, rpb_sem, sg_sem, rg_sem,
    ):
        w = lax.axis_index("win")
        t = lax.axis_index("tile")
        tiles = lax.axis_size("tile")
        off_x = (1, tiles // 4)
        off_y = (2, tiles // 2)

        def fwd(off):
            return lax.rem(t + off, tiles)

        def bwd(off):
            return lax.rem(t + tiles - off, tiles)

        def win_of(r):
            return lax.rem(w + r, windows)

        loads = [
            pltpu.make_async_copy(cx_h.at[0, 0], cxb, in_sem.at[0]),
            pltpu.make_async_copy(cy_h.at[0, 0], cyb, in_sem.at[1]),
            pltpu.make_async_copy(ker_h, kp.at[0], in_sem.at[2]),
            pltpu.make_async_copy(pro_h, kp.at[1], in_sem.at[3]),
            pltpu.make_async_copy(emi_h.at[0], sq.at[0], in_sem.at[4]),
            pltpu.make_async_copy(obs_h.at[0, 0], sq.at[1], in_sem.at[5]),
            pltpu.make_async_copy(pre_h.at[0, 0], sq.at[2], in_sem.at[6]),
        ]
        tiles_of = rows // 8
        fields = []
        for i in range(tiles_of):
            some = pl.ds(8 * NV * i, NV * min(8, levels - 8 * i))
            fields.append(pltpu.make_async_copy(init_h.at[some, :], qi.at[some, :], in_sem.at[7 + i]))
        for load in fields + loads:
            load.start()

        barrier = pltpu.get_barrier_semaphore()
        partners = []
        beside = {1, tiles // 4, tiles - 1, tiles - tiles // 4}
        for off in sorted(beside | {2, tiles - 2, tiles // 2}):
            partners.append((w, fwd(off)))
        for r in range(1, windows):
            for off in sorted(beside | {0}):
                partners.append((win_of(r), fwd(off)))
        for who in partners:
            pl.semaphore_signal(barrier, inc=1, device_id=who, device_id_type=MESH)

        lane = lanes_of((rows, LANES))
        l64 = lane & (SIDE - 1)
        low = lane < SIDE
        lane8 = lanes_of((8, LANES))
        l64_8 = lane8 & (SIDE - 1)
        low8 = lane8 < SIDE
        lane1 = lanes_of((1, LANES))
        low1 = lane1 < SIDE

        row_index = lax.broadcasted_iota(I32, (256, LANES), 0)

        def rows_key(kind):
            key, valid = (slot_key if kind == 0 else north_key)(row_index)
            return jnp.where(valid, key, -1000)

        def cols_key(kind, half):
            key, valid = (slot_key if kind == 0 else north_key)(lane1 + half * LANES)
            return jnp.where(valid, key, -2000)

        def choices(base, offs):
            out_ = []
            for off in offs:
                to = fwd(off)
                mine = (edges[base, to] == t).astype(I32)
                code = edges[base + 1, to]
                flip = edges[base + 2, to]
                out_.append((63 * flip, 4096 * (1 - mine * (1 - code)), 4096 * (1 - mine * code)))
            return out_

        row_keys = (rows_key(0), rows_key(1))

        def hot(mask):
            return jnp.where(mask, 1.0, 0.0).astype(BF16)

        def build(mat, base, offs, kind, transposed):
            for d, (flip, not_east, not_north) in enumerate(choices(base, offs)):
                for src in range(2):
                    away = not_east if src == 0 else not_north
                    for half in range(2):
                        if transposed:
                            cols = (cols_key(src, half) ^ flip) + away
                            mat[pl.ds(d * 256, 256), pl.ds(src * 256 + half * LANES, LANES)] = hot(row_keys[kind] == cols)
                        else:
                            cols = (cols_key(kind, half) ^ flip) + away
                            mat[pl.ds(src * 256, 256), pl.ds(d * 256 + half * LANES, LANES)] = hot(row_keys[src] == cols)

        def permute(x, mat):
            top = x.astype(BF16).astype(F32)
            both = jnp.concatenate([top, x - top], axis=0).astype(BF16)
            res = jnp.dot(both, mat[...], preferred_element_type=F32)
            n = x.shape[0]
            return res[:n] + res[n:]

        def send(stage, d, to):
            copy = pltpu.make_async_remote_copy(
                src_ref=sbuf.at[stage, d], dst_ref=rbuf.at[stage, d],
                send_sem=s_sem.at[stage, d], recv_sem=r_sem.at[stage, d],
                device_id=(w, to), device_id_type=MESH,
            )
            copy.start()
            return copy

        pending = []

        def send_strips(stage, east, north, mat, offs):
            res = permute(jnp.concatenate([east, north], axis=1), mat)
            copies = []
            for d in range(2):
                sbuf[stage, d] = res[:, d * 256 : (d + 1) * 256]
            for d in range(2):
                copies.append(send(stage, d, fwd(offs[d])))
            pending.extend(copies)
            return copies

        pairs, odd = tiles_of // 2, tiles_of % 2
        fold = odd == 1 and 0 < levels % 8 <= 4
        packed = 8 * (tiles_of + pairs + (odd == 1 and not fold))
        sub8 = lax.broadcasted_iota(I32, (8, LANES), 0)

        def squeeze(x):
            far, near_two = x[:, :LANES], x[:, LANES:]
            pieces = [near_two[8 * i : 8 * i + 8] for i in range(tiles_of)]
            extra = [
                jnp.where(low8, roll(far[16 * i : 16 * i + 8], SIDE), far[16 * i + 8 : 16 * i + 16]) for i in range(pairs)
            ]
            if odd:
                tail = roll(far[rows - 8 :], SIDE)
                if fold:
                    pieces[-1] = jnp.where(sub8 < 4, pieces[-1], pltpu.roll(tail, 4, 0))
                else:
                    extra.append(tail)
            return jnp.concatenate(pieces + extra, axis=0)

        def unsqueeze(x):
            near_two = [x[8 * i : 8 * i + 8] for i in range(tiles_of)]
            far = []
            for i in range(pairs):
                both_ = x[rows + 8 * i : rows + 8 * i + 8]
                far += [both_, roll(both_, SIDE)]
            if odd:
                if fold:
                    far.append(jnp.where(sub8 < 4, pltpu.roll(near_two[-1], 4, 0), 0.0))
                    near_two[-1] = jnp.where(sub8 < 4, near_two[-1], 0.0)
                else:
                    far.append(x[rows + 8 * pairs : rows + 8 * pairs + 8])
            return jnp.concatenate(near_two, axis=0), jnp.concatenate(far, axis=0)

        def received(copies, stage):
            for copy in copies:
                copy.wait_recv()
            return rbuf[stage, 0] + rbuf[stage, 1]

        def roll2(x, shift):
            return jnp.concatenate([roll(x[:, :LANES], shift), roll(x[:, LANES:], shift)], axis=1)

        slot8 = jnp.where((l64_8 & 3) < 3, l64_8 >> 2, -1)

        def put(acc, x, v, first):
            return jnp.where(slot8 == v % 16, roll(x, 4 * (v % 16) - first), acc)

        def tile_rows(i):
            if isinstance(i, int):
                return pl.ds(8 * i, 8)
            return pl.ds(pl.multiple_of(8 * i, 8), 8)

        def pack_group(src, g, first, pad, us, start):
            acc = start
            for u in us:
                moved = roll(src[:, chunk(16 * g + u + pad)], 4 * u - first)
                acc = jnp.where(((l64 >> 2) == u) & ((l64 & 3) < 3), moved, acc)
            return acc

        def pack(dst, src, first, pad):
            for g in range(2):
                dst[:, pl.ds(g * LANES, LANES)] = pack_group(src, g, first, pad, range(16), jnp.zeros((rows, LANES), F32))

        build(wx, 0, off_x, 0, False)
        if levels < rows:
            qi[pl.ds(levels * NV, (rows - levels) * NV), :] = jnp.zeros(((rows - levels) * NV, LANES), F32)
        for i in range(tiles_of):
            fields[i].wait()
            acc = [jnp.zeros((8, LANES), F32)] * 2
            for v in range(NV):
                here = qi[pl.ds(8 * NV * i + v, 8, stride=NV), :]
                q[tile_rows(i), chunk(v)] = here
                acc[v // 16] = put(acc[v // 16], here, v, 61)
            epack[tile_rows(i), pl.ds(0, LANES)] = acc[0]
            epack[tile_rows(i), pl.ds(LANES, LANES)] = acc[1]

        strips = permute(jnp.concatenate([epack[...], q[:, pl.ds(CELLS - 256, 256)]], axis=1), wx)
        for d in range(2):
            sbuf[0, d] = strips[:, d * 256 : (d + 1) * 256]
        pl.semaphore_wait(barrier, len(partners))
        first = [send(0, d, fwd(off_x[d])) for d in range(2)]
        pending.extend(first)
        build(wy, 3, off_y, 1, False)

        def widen(c, cb):
            c[pl.ds(levels, rows - levels), :] = jnp.zeros((rows - levels, CELLS), F32)

            @pl.loop(0, NV // 8)
            def _(v):
                some = pl.ds(pl.multiple_of(v * 8 * LANES, 8 * LANES), 8 * LANES)
                c[pl.ds(0, levels), some] = cb[:, some].astype(F32)

        loads[0].wait()
        widen(cx, cxb)

        def x_interior():
            @pl.loop(0, tiles_of)
            def _(i):
                here_rows = tile_rows(i)
                ewrap[here_rows, :] = roll2(epack[here_rows, :], SIDE)
                acc = [jnp.zeros((8, LANES), F32)] * 2
                for v in range(NV):
                    here = q[here_rows, chunk(v)]
                    a1, a2, a3 = coefs(cx[here_rows, chunk(v)])
                    r1, r2, r3 = roll(here, 1), roll(here, 2), roll(here, 3)
                    flux = r1 * a1 + r2 * a2 + r3 * a3
                    outlet = here * a1 + r1 * a2 + r2 * a3
                    res = here + flux - jnp.where(l64_8 == SIDE - 1, outlet, roll(flux, -1))
                    bx[here_rows, chunk(v + 2)] = res
                    acc[v // 16] = put(acc[v // 16], res, v, 61)
                epack[here_rows, pl.ds(0, LANES)] = acc[0]
                epack[here_rows, pl.ds(LANES, LANES)] = acc[1]

        loads[1].wait()
        widen(cy, cyb)
        for i in range(3):
            loads[4 + i].wait()
            x = sq[i]
            sq2[i, :, pl.ds(0, SIDE)] = x

        for i in range(3):
            x = sq2[i]
            sq2[i] = jnp.where(lanes_of((SIDE, LANES)) < SIDE, x, pltpu.roll(x, SIDE, 1))

        for i in range(3):
            @pl.loop(0, NV // 8)
            def _(k, i=i):
                for j in range(8):
                    v = k * 8 + j
                    row = jnp.where(low1, sq2[i, pl.ds(2 * v, 1), :], sq2[i, pl.ds(2 * v + 1, 1), :])
                    flat[i, :, chunk(v)] = jnp.broadcast_to(row, (8, LANES))

        loads[2].wait()
        loads[3].wait()
        diag = lax.broadcasted_iota(I32, (levels, levels), 0) == lax.broadcasted_iota(I32, (levels, levels), 1)
        for i, col in ((0, kcol), (1, pcol)):
            column = jnp.sum(jnp.where(diag, jnp.broadcast_to(kp[i], (levels, levels)), 0.0), axis=1, keepdims=True)
            col[...] = jnp.zeros((rows, LANES), F32)
            col[pl.ds(0, levels), :] = jnp.broadcast_to(column, (levels, LANES))
        inv = 1.0 / jnp.sum(kp[0], axis=1, keepdims=True)
        inv8 = jnp.broadcast_to(inv, (8, LANES))


        sset[pl.ds(0, packed), :] = squeeze(
            jnp.concatenate([roll(cy[:, chunk(1)], SIDE), cy[:, chunk(0)]], axis=1)
        )
        sset[pl.ds(packed + 4, 4), :] = jnp.zeros((4, LANES), F32)
        for i in range(2):
            for v in range(2):
                sset[pl.ds(packed + 2 * i + v, 1), :] = flat[1 + i, pl.ds(0, 1), chunk(v)]
        sets = []
        for d in range(2):
            copy = pltpu.make_async_remote_copy(
                src_ref=sset, dst_ref=rset.at[d], send_sem=sset_sem.at[d], recv_sem=rset_sem.at[d],
                device_id=(w, bwd(off_y[d])), device_id_type=MESH,
            )
            copy.start()
            sets.append(copy)

        x_interior()

        pack(cpack, cx, 0, 0)
        part = lanes_of((rows, 256)) & 3
        p1, p2, p3 = coefs(cpack[...])
        west1 = jnp.where(part == 0, p1, 0.0)
        west2 = jnp.where(part <= 1, p2, 0.0)
        west3 = jnp.where(part <= 2, p3, 0.0)
        cpack3 = (west1, west2, west3)

        def west_change(panel):
            panel = panel - ewrap[...]
            f = panel * cpack3[2] + roll2(panel, -1) * cpack3[1] + roll2(panel, -2) * cpack3[0]
            return jnp.where(part < 3, f - roll2(f, -1), 0.0)

        def y_flux(qv_r, q1, q1_r, q2_r, c):
            a1, a2, a3 = coefs(c)
            s1 = jnp.where(low, q1_r, qv_r)
            return s1 * a1 + q1 * a2 + jnp.where(low, q2_r, q1_r) * a3

        def y_interior(here_rows, finish, changed):
            none = jnp.zeros((8, LANES), F32)
            xs, rs, turned, outlet = {-1: none, -2: none}, {-1: none, -2: none}, {}, None
            done = {}
            lowest = 2 if changed else 0
            for v in range(NV):
                xs[v] = bx[here_rows, chunk(v + 2)]
                if changed:
                    change = dbuf[here_rows, pl.ds(v // 16 * LANES, LANES)]
                    xs[v] = xs[v] + jnp.where(l64_8 < 3, roll(change, -4 * (v % 16)), 0.0)
                    if v < 3:
                        bx[here_rows, chunk(v + 2)] = xs[v]
                rs[v] = roll(xs[v], SIDE)
                if v < lowest:
                    continue
                a1, a2, a3 = coefs(cy[here_rows, chunk(v)])
                flux = jnp.where(low8, rs[v - 1], rs[v]) * a1 + xs[v - 1] * a2 + jnp.where(low8, rs[v - 2], rs[v - 1]) * a3
                turned[v] = roll(flux, SIDE)
                done[v] = xs[v] + flux
                if v > lowest:
                    finish(v - 1, done[v - 1] - jnp.where(low8, turned[v - 1], turned[v]))
                if v == NV - 1:
                    outlet = xs[v] * a1 + jnp.where(low8, rs[v - 1], rs[v]) * a2 + xs[v - 1] * a3
                    finish(v, done[v] - jnp.where(low8, turned[v], outlet))

        def y_first(ta, pb):
            q0_, q1_, q2_ = bx[:, chunk(2)], bx[:, chunk(3)], bx[:, chunk(4)]
            t0, t1, t2 = roll(q0_, SIDE), roll(q1_, SIDE), roll(q2_, SIDE)
            tb = roll(pb, SIDE)
            above = roll(y_flux(t2, q1_, t1, t0, cy[:, chunk(2)]), SIDE)
            f1 = y_flux(t1, q0_, t0, tb, cy[:, chunk(1)])
            f0 = y_flux(t0, pb, tb, ta, cy[:, chunk(0)])
            g1, g0 = roll(f1, SIDE), roll(f0, SIDE)
            n1 = q1_ + f1 - jnp.where(low, g1, above) + emitted(1)
            n0 = q0_ + f0 - jnp.where(low, g0, g1) + emitted(0)
            return n0, n1

        def emitted(v):
            return pcol[...] * jnp.concatenate([flat[0, :, chunk(v)]] * (rows // 8), axis=0)

        def sum_levels(x):
            acc = x[0:8]
            for i in range(1, rows // 8):
                acc = acc + x[8 * i : 8 * i + 8]
            return acc

        def down(x):
            return jnp.broadcast_to(jnp.sum(x, axis=0, keepdims=True), (8, LANES))

        def tall(x):
            return jnp.concatenate([x] * (rows // 8), axis=0)

        panel = received(first, 0)
        dbuf[...] = west_change(panel)
        change = dbuf[:, pl.ds(LANES, LANES)]
        ends_now = [
            bx[:, chunk(v + 2)] + jnp.where(l64 < 3, roll(change, -4 * (v % 16)), 0.0) for v in (NV - 2, NV - 1)
        ]
        res = permute(jnp.concatenate([epack[...]] + ends_now, axis=1), wy)
        for d in range(2):
            sy[d] = squeeze(res[:, d * 256 : (d + 1) * 256])
        y1 = []
        for d in range(2):
            copy = pltpu.make_async_remote_copy(
                src_ref=sy.at[d], dst_ref=ry.at[d], send_sem=s_sem.at[1, d], recv_sem=r_sem.at[1, d],
                device_id=(w, fwd(off_y[d])), device_id_type=MESH,
            )
            copy.start()
            y1.append(copy)
        pending.extend(y1)

        @pl.loop(0, tiles_of)
        def _(i):
            here_rows = tile_rows(i)
            acc = [jnp.zeros((8, LANES), F32)] * 2
            share = pcol[here_rows, :]

            def finish(v, res):
                res = res + share * flat[0, :, chunk(v)]
                q[here_rows, chunk(v)] = res
                acc[v // 16] = put(acc[v // 16], res, v, 61)

            y_interior(here_rows, finish, True)
            epack[here_rows, pl.ds(0, LANES)] = acc[0]
            epack[here_rows, pl.ds(LANES, LANES)] = acc[1]

        build(wyt, 3, off_y, 1, True)
        build(wxt, 0, off_x, 0, True)
        pack(cyp, cy, 0, 0)
        for copy in y1:
            copy.wait_recv()
        near_two, far_one = unsqueeze(ry[0] + ry[1])
        east = epack[:, pl.ds(0, LANES)]
        for v, res in enumerate(y_first(far_one, near_two)):
            q[:, chunk(v)] = res
            east = jnp.where(((l64 >> 2) == v) & ((l64 & 3) < 3), roll(res, 4 * v - 61), east)
        epack[:, pl.ds(0, LANES)] = east

        x2 = send_strips(2, epack[...], q[:, pl.ds(CELLS - 256, 256)], wx, off_x)
        x_interior()
        for copy in sets:
            copy.wait_recv()

        gf[...] = jnp.zeros((8, CELLS), F32)

        @pl.loop(0, tiles_of)
        def _(i):
            here_rows = tile_rows(i)
            share, weight = pcol[here_rows, :], kcol[here_rows, :]

            def finish(v, res):
                gf[:, chunk(v)] = gf[:, chunk(v)] + (res + share * flat[0, :, chunk(v)]) * weight

            y_interior(here_rows, finish, False)

        def slots(x):
            index = lanes_of(x.shape)
            return (index >> 6) & 1, (index >> 2) & 15

        def shift_down(x):
            high, u = slots(x[0])
            res = []
            for g in range(2):
                over = roll(x[g - 1], 4) if g > 0 else jnp.zeros_like(x[0])
                res.append(jnp.where(high == 1, roll(x[g], SIDE), jnp.where(u == 0, over, roll(x[g], 68))))
            return res

        def shift_down2(x):
            u = slots(x[0])[1]
            res = []
            for g in range(2):
                over = roll(x[g - 1], 68) if g > 0 else jnp.zeros_like(x[0])
                res.append(jnp.where(u == 0, over, roll(x[g], 4)))
            return res

        def shift_up(x, after):
            high, u = slots(x[0])
            res = []
            for g in range(2):
                over = roll(x[g + 1], 124) if g == 0 else after
                res.append(jnp.where(high == 0, roll(x[g], SIDE), jnp.where(u == 15, over, roll(x[g], 60))))
            return res

        ca = [coefs(cyp[:, pl.ds(g * LANES, LANES)]) for g in range(2)]
        k_all = kcol[...]
        zero = jnp.zeros((rows, LANES), F32)

        panel = received(x2, 2)
        dbuf[...] = west_change(panel)
        change = dbuf[:, pl.ds(LANES, LANES)]
        ends_now = [
            bx[:, chunk(v + 2)] + jnp.where(l64 < 3, roll(change, -4 * (v % 16)), 0.0) for v in (NV - 2, NV - 1)
        ]
        panels = permute(jnp.concatenate([epack[...]] + ends_now, axis=1), wy)

        def misfit_weight(col, v_obs, v_pre):
            return v_pre * (col * inv8 - v_obs) * inv8

        new = [dbuf[:, pl.ds(g * LANES, LANES)] for g in range(2)]
        s1, s2 = shift_down(new), shift_down2(new)
        s3 = shift_down(s2)
        flow = [s1[g] * ca[g][0] + s2[g] * ca[g][1] + s3[g] * ca[g][2] for g in range(2)]
        out_flow = shift_up(flow, new[1] * ca[1][0] + s1[1] * ca[1][1] + s2[1] * ca[1][2])
        gained = [sum_levels((new[g] + flow[g] - out_flow[g]) * k_all) for g in range(2)]

        def column(v):
            return down(gf[:, chunk(v)] + jnp.where(l64_8 < 3, roll(gained[v // 16], -4 * (v % 16)), 0.0))

        for v in range(2):
            scol[:, chunk(v)] = column(v)[0:1]
        cols = []
        for d in range(2):
            copy = pltpu.make_async_remote_copy(
                src_ref=scol, dst_ref=rcol.at[d], send_sem=scol_sem.at[d], recv_sem=rcol_sem.at[d],
                device_id=(w, bwd(off_y[d])), device_id_type=MESH,
            )
            copy.start()
            cols.append(copy)

        effects, edge = [], []
        for d in range(2):
            pa, pb = panels[:, d * 256 : d * 256 + LANES], panels[:, d * 256 + LANES : d * 256 + 256]
            ra, rb = roll(pa, SIDE), roll(pb, SIDE)
            c0, c1 = unsqueeze(rset[d, pl.ds(0, packed), :])
            z1, z2, z3 = coefs(c0)
            o3 = coefs(c1)[2]
            edge.append((z1, z2, z3, o3))
            h0 = jnp.where(low, rb, 0.0) * z1 + pb * z2 + jnp.where(low, ra, rb) * z3
            h1 = jnp.where(low, rb, 0.0) * o3
            k0, k1 = roll(h0, SIDE), roll(h1, SIDE)
            d0 = h0 - jnp.where(low, k0, k1)
            d1 = h1 - jnp.where(low, k1, 0.0)
            effects.append((down(sum_levels(d0 * k_all)), down(sum_levels(d1 * k_all))))
            for v in range(2):
                sdc[d, :, chunk(v)] = effects[d][v][0:1]
        for d in range(2):
            copy = pltpu.make_async_remote_copy(
                src_ref=sdc.at[d], dst_ref=rdc.at[d], send_sem=s_sem.at[3, d], recv_sem=r_sem.at[3, d],
                device_id=(w, fwd(off_y[d])), device_id_type=MESH,
            )
            copy.start()
            pending.append(copy)

        def weigh(v, col):
            gf[:, chunk(v)] = misfit_weight(col, flat[1, :, chunk(v)], flat[2, :, chunk(v)])

        def slope(v):
            here = gf[:, chunk(v)]
            before = roll(gf[:, chunk(v - 1)], SIDE) if v > 0 else jnp.zeros((8, LANES), F32)
            return here - jnp.where(low8, before, roll(here, SIDE))

        for v in range(2, NV):
            weigh(v, column(v))
        gf[:, pl.ds(0, 256)] = jnp.zeros((8, 256), F32)
        for v in range(2, NV):
            df[:, chunk(v)] = slope(v)

        @pl.loop(0, tiles_of)
        def _(i):
            here_rows = tile_rows(i)
            weight = kcol[here_rows, :]
            none = jnp.zeros((8, LANES), F32)
            top = -weight * roll(gf[:, chunk(NV - 1)], SIDE)
            b1, b2, b3 = coefs(roll(cy[here_rows, chunk(NV - 1)], SIDE))
            first_up = roll(jnp.where(low8, top * b1, 0.0), SIDE)
            second_up = jnp.where(low8, top * b2, 0.0)
            third_up, third_up2 = roll(jnp.where(low8, top * b3, 0.0), SIDE), none
            acc = [none, none]
            for v in range(NV - 1, 1, -1):
                bar = weight * df[:, chunk(v)]
                a1, a2, a3 = coefs(cy[here_rows, chunk(v)])
                turned1, turned3 = roll(bar * a1, SIDE), roll(bar * a3, SIDE)
                res = (
                    weight * gf[:, chunk(v)]
                    + jnp.where(low8, turned1, first_up)
                    + second_up
                    + jnp.where(low8, third_up, third_up2)
                )
                mu[here_rows, chunk(v)] = res
                if v < NV - 2:
                    acc[v // 16] = put(acc[v // 16], res, v, 0)
                first_up, second_up, third_up, third_up2 = turned1, bar * a2, turned3, third_up
            dbuf[here_rows, pl.ds(0, LANES)] = acc[0]
            dbuf[here_rows, pl.ds(LANES, LANES)] = acc[1]

        bars = []
        for d in range(2):
            cols[d].wait_recv()
            z1, z2, z3, o3 = edge[d]
            w0, w1 = (
                misfit_weight(
                    jnp.broadcast_to(rcol[d, :, chunk(v)], (8, LANES)) + effects[d][v],
                    jnp.broadcast_to(rset[d, pl.ds(packed + v, 1), :], (8, LANES)),
                    jnp.broadcast_to(rset[d, pl.ds(packed + 2 + v, 1), :], (8, LANES)),
                )
                for v in range(2)
            )
            turned = roll(w0, SIDE)
            bar0 = k_all * tall(w0 - jnp.where(low8, 0.0, turned))
            bar1 = k_all * tall(w1 - jnp.where(low8, turned, roll(w1, SIDE)))
            third0, third1 = roll(bar0 * z3, SIDE), roll(bar1 * o3, SIDE)
            near_rows = jnp.where(low, 0.0, roll(bar0 * z1, SIDE)) + bar0 * z2 + jnp.where(low, third0, third1)
            far_rows = jnp.where(low, 0.0, third0)
            bars.append(jnp.concatenate([far_rows, near_rows], axis=1))
        back = permute(jnp.concatenate(bars, axis=1), wyt)
        back_east, back_north = back[:, :256], back[:, 256:]

        for copy in pending[-2:]:
            copy.wait_recv()
        for v in range(2):
            weigh(v, jnp.broadcast_to(scol[:, chunk(v)] + rdc[0, :, chunk(v)] + rdc[1, :, chunk(v)], (8, LANES)))
        made = {}
        for v in range(4):
            bar = k_all * tall(slope(v))
            a1, a2, a3 = coefs(cy[:, chunk(v)])
            made[v] = (roll(bar * a1, SIDE), bar * a2, roll(bar * a3, SIDE))
        for v in range(2):
            mu[:, chunk(v)] = (
                k_all * tall(gf[:, chunk(v)])
                + jnp.where(low, made[v][0], made[v + 1][0])
                + made[v + 1][1]
                + jnp.where(low, made[v + 1][2], made[v + 2][2])
            )
        mu[:, pl.ds(CELLS - 256, 256)] = mu[:, pl.ds(CELLS - 256, 256)] + back_north
        west0 = pack_group(mu, 0, 0, 0, range(2), dbuf[:, pl.ds(0, LANES)])
        west1_ = pack_group(mu, 1, 0, 0, range(14, 16), dbuf[:, pl.ds(LANES, LANES)])
        west = jnp.concatenate([west0, west1_], axis=1)
        diff = west - jnp.where(part > 0, roll2(west, 1), 0.0)
        pbar = diff * cpack3[2] + roll2(diff * cpack3[1], 1) + roll2(diff * cpack3[0], 2)
        p_all = pcol[...]
        for v in range(2):
            spb[:, chunk(v)] = down(sum_levels(pbar[:, v * LANES : (v + 1) * LANES] * p_all))[0:1]
        finals = []
        for r in range(windows):
            for d in range(2):
                copy = pltpu.make_async_remote_copy(
                    src_ref=spb, dst_ref=rpb.at[d, r], send_sem=spb_sem.at[d, r], recv_sem=rpb_sem.at[d, r],
                    device_id=(win_of(r), bwd(off_x[d])), device_id_type=MESH,
                )
                copy.start()
                finals.append(copy)

        bfix[...] = back_east
        both = jnp.broadcast_to(jnp.sum(kcol[...] * pcol[...], axis=0, keepdims=True), (8, LANES))
        sums = []
        for r in [*range(1, windows), 0]:
            to = win_of(r)
            side = lax.div(to * per, 16)
            east = bfix[:, chunk(side)]
            if per < 16:
                east = jnp.where(lax.rem(to * per, 16) == 8, roll(east, -32), east)
            for k in range(per):
                v = to * per + k
                whole = mu[:, chunk(v)] + jnp.where(l64 >= 61, roll(east, 61 - 4 * k), 0.0)
                m = whole * p_all
                c = cx[:, chunk(v)]
                a1, a2, a3 = coefs(jnp.where(l64 == 0, roll(c, 1), c))
                f = jnp.where(l64 == 0, 0.0, m) - roll(m, 1)
                s0 = sum_levels(m)
                s1, s2, s3 = sum_levels(f * a1), sum_levels(f * a2), sum_levels(f * a3)
                res = s0 + roll(s1, -1) + jnp.where(l64_8 < 63, roll(s2, -2), 0.0) + jnp.where(l64_8 < 62, roll(s3, -3), 0.0)
                gint[r, pl.ds(k, 1), :] = (down(res) + both * gf[:, chunk(v)])[0:1]
            if r > 0:
                copy = pltpu.make_async_remote_copy(
                    src_ref=gint.at[r], dst_ref=rg.at[r - 1],
                    send_sem=sg_sem.at[r - 1], recv_sem=rg_sem.at[r - 1],
                    device_id=(to, t), device_id_type=MESH,
                )
                copy.start()
                sums.append(copy)

        for copy in finals:
            copy.wait_recv()
        halves = []
        for d in range(2):
            acc = rpb[d, 0]
            for r in range(1, windows):
                acc = acc + rpb[d, r]
            halves.append(jnp.broadcast_to(acc, (8, 256)))
        ends = permute(jnp.concatenate(halves, axis=1), wxt)
        for v in range(NV):
            g, u = v // 16, v % 16
            row = jnp.where(l64_8 >= 61, roll(ends[:, g * LANES : (g + 1) * LANES], 61 - 4 * u), 0.0)
            if v >= NV - 2:
                at = 256 + (v - NV + 2) * LANES
                row = row + ends[:, at : at + LANES]
            fin[pl.ds(v, 1), :] = row[0:1]
        mine = pl.ds(pl.multiple_of(w * per, per), per)
        total = gint[0] + fin[mine, :]
        for copy in sums:
            copy.wait_recv()
        for r in range(1, windows):
            total = total + rg[r - 1]
        out[0, pl.ds(0, per, stride=2), :] = total[:, :SIDE]
        out[0, pl.ds(1, per, stride=2), :] = pltpu.roll(total, SIDE, 1)[:, :SIDE]

        for copy in pending + sets + cols + finals + sums:
            copy.wait_send()

    return kernel, rows, per


def body(initial, courant_x, courant_y, observed, precision_w, kernel, profile, emission, edges):
    levels = initial.shape[2]
    windows = lax.axis_size("win")
    run, rows, per = make_kernel(levels, windows)
    tiles_of = rows // 8
    packed = 8 * (tiles_of + tiles_of // 2 + (tiles_of % 2 == 1 and not 0 < levels % 8 <= 4))
    vm = pltpu.VMEM
    dma = pltpu.SemaphoreType.DMA
    anywhere = pl.BlockSpec(memory_space=pl.ANY)
    return pl.pallas_call(
        run,
        out_shape=pltpu.VMEM((1, 2 * per, SIDE), F32),
        in_specs=[anywhere] * 8 + [pl.BlockSpec(memory_space=pltpu.SMEM)],
        out_specs=pl.BlockSpec(memory_space=pltpu.VMEM),
        scratch_shapes=[
            vm((rows * NV, LANES), F32),
            vm((rows, CELLS), F32),
            vm((rows, CELLS + 256), F32),
            vm((rows, CELLS), F32),
            vm((rows, CELLS), F32),
            vm((rows, CELLS), F32),
            vm((levels, CELLS), BF16),
            vm((levels, CELLS), BF16),
            vm((3, SIDE, SIDE), F32),
            vm((3, SIDE, LANES), F32),
            vm((3, 8, CELLS), F32),
            vm((2, 1, levels), F32),
            vm((rows, LANES), F32),
            vm((rows, LANES), F32),
            vm((8, CELLS), F32),
            vm((8, CELLS), F32),
            vm((rows, 256), F32),
            vm((512, 512), BF16),
            vm((512, 512), BF16),
            vm((512, 512), BF16),
            vm((512, 512), BF16),
            vm((rows, 256), F32),
            vm((rows, 256), F32),
            vm((rows, 256), F32),
            vm((rows, 256), F32),
            vm((rows, 256), F32),
            vm((4, 2, rows, 256), F32),
            vm((4, 2, rows, 256), F32),
            vm((2, packed, LANES), F32),
            vm((2, packed, LANES), F32),
            vm((2, 1, 256), F32),
            vm((2, 1, 256), F32),
            vm((packed + 8, LANES), F32),
            vm((2, packed + 8, LANES), F32),
            vm((1, 256), F32),
            vm((2, 1, 256), F32),
            vm((1, 256), F32),
            vm((2, windows, 1, 256), F32),
            vm((windows, per, LANES), F32),
            vm((windows - 1, per, LANES), F32),
            vm((NV, LANES), F32),
            dma((7 + rows // 8,)),
            dma((4, 2)),
            dma((4, 2)),
            dma((2,)),
            dma((2,)),
            dma((2,)),
            dma((2,)),
            dma((2, windows)),
            dma((2, windows)),
            dma((windows - 1,)),
            dma((windows - 1,)),
        ],
        compiler_params=pltpu.CompilerParams(collective_id=0, has_side_effects=True),
    )(
        initial.reshape(levels * NV, LANES), courant_x, courant_y, observed, precision_w,
        kernel.reshape(1, levels), profile.reshape(1, levels), emission, edges,
    )


def solution(mesh):
    placed = (
        P("win", "tile", None, None),
        P("win", "tile", None, None),
        P("win", "tile", None, None),
        P("win", "tile", None, None),
        P("win", "tile", None, None),
        P(),
        P(),
        P("tile", None, None),
        P(),
    )
    return jax.shard_map(
        body, mesh=mesh, in_specs=placed, out_specs=P("tile", "win", None), check_vma=False
    )
```

```python
import jax
import jax.numpy as jnp
from jax import lax
from jax.experimental import pallas as pl
from jax.experimental.pallas import tpu as pltpu
from jax.sharding import PartitionSpec as P

F32 = jnp.float32
BF16 = jnp.bfloat16
I32 = jnp.int32
SIDE = 64
LANES = 128
CELLS = SIDE * SIDE
NV = CELLS // LANES
MESH = pl.DeviceIdType.MESH


def roll(x, shift):
    return pltpu.roll(x, shift % LANES, 1)


def lanes_of(shape):
    return lax.broadcasted_iota(I32, shape, 1)


def coefs(c):
    one, three = jnp.minimum(c, 1.0), jnp.maximum(c - 2.0, 0.0)
    return one, c - one - three, three


def chunk(v):
    if isinstance(v, int):
        return pl.ds(v * LANES, LANES)
    return pl.ds(pl.multiple_of(v * LANES, LANES), LANES)


def slot_key(index):
    part = index & 3
    cell = 32 * (index >> 7) + 2 * ((index >> 2) & 15) + ((index >> 6) & 1)
    return part * SIDE + cell, part < 3


def north_key(index):
    return index - SIDE, index >= SIDE


def make_kernel(levels, windows):
    rows = (levels + 7) // 8 * 8
    per = NV // windows

    def kernel(
        init_h, cx_h, cy_h, obs_h, pre_h, ker_h, pro_h, emi_h, edges,
        out,
        qi, q, bx, mu, cx, cy, cxb, cyb, sq, sq2, flat, kp, kcol, pcol, gf, df, bfix,
        wx, wxt, wy, wyt, epack, ewrap, cyp, cpack, dbuf,
        sbuf, rbuf, sy, ry, sdc, rdc, sset, rset, scol, rcol, spb, rpb, gint, rg, fin,
        in_sem, s_sem, r_sem, sset_sem, rset_sem, scol_sem, rcol_sem, spb_sem, rpb_sem, sg_sem, rg_sem,
    ):
        w = lax.axis_index("win")
        t = lax.axis_index("tile")
        tiles = lax.axis_size("tile")
        off_x = (1, tiles // 4)
        off_y = (2, tiles // 2)

        def fwd(off):
            return lax.rem(t + off, tiles)

        def bwd(off):
            return lax.rem(t + tiles - off, tiles)

        def win_of(r):
            return lax.rem(w + r, windows)

        loads = [
            pltpu.make_async_copy(cx_h.at[0, 0], cxb, in_sem.at[0]),
            pltpu.make_async_copy(cy_h.at[0, 0], cyb, in_sem.at[1]),
            pltpu.make_async_copy(ker_h, kp.at[0], in_sem.at[2]),
            pltpu.make_async_copy(pro_h, kp.at[1], in_sem.at[3]),
            pltpu.make_async_copy(emi_h.at[0], sq.at[0], in_sem.at[4]),
            pltpu.make_async_copy(obs_h.at[0, 0], sq.at[1], in_sem.at[5]),
            pltpu.make_async_copy(pre_h.at[0, 0], sq.at[2], in_sem.at[6]),
        ]
        tiles_of = rows // 8
        fields = []
        for i in range(tiles_of):
            some = pl.ds(8 * NV * i, NV * min(8, levels - 8 * i))
            fields.append(pltpu.make_async_copy(init_h.at[some, :], qi.at[some, :], in_sem.at[7 + i]))
        for load in fields + loads:
            load.start()

        barrier = pltpu.get_barrier_semaphore()
        partners = []
        beside = {1, tiles // 4, tiles - 1, tiles - tiles // 4}
        for off in sorted(beside | {2, tiles - 2, tiles // 2}):
            partners.append((w, fwd(off)))
        for r in range(1, windows):
            for off in sorted(beside | {0}):
                partners.append((win_of(r), fwd(off)))
        for who in partners:
            pl.semaphore_signal(barrier, inc=1, device_id=who, device_id_type=MESH)

        lane = lanes_of((rows, LANES))
        l64 = lane & (SIDE - 1)
        low = lane < SIDE
        lane8 = lanes_of((8, LANES))
        l64_8 = lane8 & (SIDE - 1)
        low8 = lane8 < SIDE
        lane1 = lanes_of((1, LANES))
        low1 = lane1 < SIDE

        row_index = lax.broadcasted_iota(I32, (256, LANES), 0)

        def rows_key(kind):
            key, valid = (slot_key if kind == 0 else north_key)(row_index)
            return jnp.where(valid, key, -1000)

        def cols_key(kind, half):
            key, valid = (slot_key if kind == 0 else north_key)(lane1 + half * LANES)
            return jnp.where(valid, key, -2000)

        def choices(base, offs):
            out_ = []
            for off in offs:
                to = fwd(off)
                mine = (edges[base, to] == t).astype(I32)
                code = edges[base + 1, to]
                flip = edges[base + 2, to]
                out_.append((63 * flip, 4096 * (1 - mine * (1 - code)), 4096 * (1 - mine * code)))
            return out_

        row_keys = (rows_key(0), rows_key(1))

        def hot(mask):
            return jnp.where(mask, 1.0, 0.0).astype(BF16)

        def build(mat, base, offs, kind, transposed):
            for d, (flip, not_east, not_north) in enumerate(choices(base, offs)):
                for src in range(2):
                    away = not_east if src == 0 else not_north
                    for half in range(2):
                        if transposed:
                            cols = (cols_key(src, half) ^ flip) + away
                            mat[pl.ds(d * 256, 256), pl.ds(src * 256 + half * LANES, LANES)] = hot(row_keys[kind] == cols)
                        else:
                            cols = (cols_key(kind, half) ^ flip) + away
                            mat[pl.ds(src * 256, 256), pl.ds(d * 256 + half * LANES, LANES)] = hot(row_keys[src] == cols)

        def permute(x, mat, first=0):
            top = x.astype(BF16).astype(F32)
            both = jnp.concatenate([top, x - top], axis=0).astype(BF16)
            res = jnp.dot(both, mat[pl.ds(first, x.shape[1]), :], preferred_element_type=F32)
            n = x.shape[0]
            return res[:n] + res[n:]

        def roll2(x, shift):
            return jnp.concatenate([roll(x[:, :LANES], shift), roll(x[:, LANES:], shift)], axis=1)

        hide = tiles_of >= 4 and 0 < levels % 8 <= 4

        def tuck(x):
            if not hide:
                return x
            free = (lanes_of((8, 256)) & 3) == 3
            tail = x[rows - 8 :]
            heads = [jnp.where(free, roll2(tail, 3 - i), x[8 * i : 8 * i + 8]) for i in range(3)]
            return jnp.concatenate(heads + [x[24 : rows - 8]], axis=0)

        def untuck(x):
            if not hide:
                return x
            place = lanes_of((8, 256)) & 3
            tail = jnp.zeros((8, 256), F32)
            for i in range(3):
                tail = jnp.where(place == i, roll2(x[8 * i : 8 * i + 8], i - 3), tail)
            return jnp.concatenate([x, tail], axis=0)

        def send(stage, d, to):
            copy = pltpu.make_async_remote_copy(
                src_ref=sbuf.at[stage, d], dst_ref=rbuf.at[stage, d],
                send_sem=s_sem.at[stage, d], recv_sem=r_sem.at[stage, d],
                device_id=(w, to), device_id_type=MESH,
            )
            copy.start()
            return copy

        pending = []

        pairs, odd = tiles_of // 2, tiles_of % 2
        fold = odd == 1 and 0 < levels % 8 <= 4
        packed = 8 * (tiles_of + pairs + (odd == 1 and not fold))
        sub8 = lax.broadcasted_iota(I32, (8, LANES), 0)

        def squeeze(x):
            far, near_two = x[:, :LANES], x[:, LANES:]
            pieces = [near_two[8 * i : 8 * i + 8] for i in range(tiles_of)]
            extra = [
                jnp.where(low8, roll(far[16 * i : 16 * i + 8], SIDE), far[16 * i + 8 : 16 * i + 16]) for i in range(pairs)
            ]
            if odd:
                tail = roll(far[rows - 8 :], SIDE)
                if fold:
                    pieces[-1] = jnp.where(sub8 < 4, pieces[-1], pltpu.roll(tail, 4, 0))
                else:
                    extra.append(tail)
            return jnp.concatenate(pieces + extra, axis=0)

        def unsqueeze(x):
            near_two = [x[8 * i : 8 * i + 8] for i in range(tiles_of)]
            far = []
            for i in range(pairs):
                both_ = x[rows + 8 * i : rows + 8 * i + 8]
                far += [both_, roll(both_, SIDE)]
            if odd:
                if fold:
                    far.append(jnp.where(sub8 < 4, pltpu.roll(near_two[-1], 4, 0), 0.0))
                    near_two[-1] = jnp.where(sub8 < 4, near_two[-1], 0.0)
                else:
                    far.append(x[rows + 8 * pairs : rows + 8 * pairs + 8])
            return jnp.concatenate(near_two, axis=0), jnp.concatenate(far, axis=0)

        def received(copies, stage):
            for copy in copies:
                copy.wait_recv()
            return untuck(rbuf[stage, 0] + rbuf[stage, 1])

        slot8 = jnp.where((l64_8 & 3) < 3, l64_8 >> 2, -1)

        def put(acc, x, v, first):
            return jnp.where(slot8 == v % 16, roll(x, 4 * (v % 16) - first), acc)

        def tile_rows(i):
            if isinstance(i, int):
                return pl.ds(8 * i, 8)
            return pl.ds(pl.multiple_of(8 * i, 8), 8)

        def pack_group(src, g, first, pad, us, start):
            acc = start
            for u in us:
                moved = roll(src[:, chunk(16 * g + u + pad)], 4 * u - first)
                acc = jnp.where(((l64 >> 2) == u) & ((l64 & 3) < 3), moved, acc)
            return acc

        def pack(dst, src, first, pad):
            for g in range(2):
                dst[:, pl.ds(g * LANES, LANES)] = pack_group(src, g, first, pad, range(16), jnp.zeros((rows, LANES), F32))

        build(wx, 0, off_x, 0, False)
        if levels < rows:
            qi[pl.ds(levels * NV, (rows - levels) * NV), :] = jnp.zeros(((rows - levels) * NV, LANES), F32)
        for i in range(tiles_of):
            fields[i].wait()
            acc = [jnp.zeros((8, LANES), F32)] * 2
            for v in range(NV):
                here = qi[pl.ds(8 * NV * i + v, 8, stride=NV), :]
                q[tile_rows(i), chunk(v)] = here
                acc[v // 16] = put(acc[v // 16], here, v, 61)
            epack[tile_rows(i), pl.ds(0, LANES)] = acc[0]
            epack[tile_rows(i), pl.ds(LANES, LANES)] = acc[1]

        strips = permute(jnp.concatenate([epack[...], q[:, pl.ds(CELLS - 256, 256)]], axis=1), wx)
        for d in range(2):
            sbuf[0, d] = tuck(strips[:, d * 256 : (d + 1) * 256])
        pl.semaphore_wait(barrier, len(partners))
        first = [send(0, d, fwd(off_x[d])) for d in range(2)]
        pending.extend(first)
        build(wy, 3, off_y, 1, False)

        def widen(c, cb):
            c[pl.ds(levels, rows - levels), :] = jnp.zeros((rows - levels, CELLS), F32)

            @pl.loop(0, NV // 8)
            def _(v):
                some = pl.ds(pl.multiple_of(v * 8 * LANES, 8 * LANES), 8 * LANES)
                c[pl.ds(0, levels), some] = cb[:, some].astype(F32)

        loads[0].wait()
        widen(cx, cxb)

        def x_interior():
            @pl.loop(0, tiles_of)
            def _(i):
                here_rows = tile_rows(i)
                ewrap[here_rows, :] = roll2(epack[here_rows, :], SIDE)
                acc = [jnp.zeros((8, LANES), F32)] * 2
                for v in range(NV):
                    here = q[here_rows, chunk(v)]
                    a1, a2, a3 = coefs(cx[here_rows, chunk(v)])
                    r1, r2, r3 = roll(here, 1), roll(here, 2), roll(here, 3)
                    flux = r1 * a1 + r2 * a2 + r3 * a3
                    outlet = here * a1 + r1 * a2 + r2 * a3
                    res = here + flux - jnp.where(l64_8 == SIDE - 1, outlet, roll(flux, -1))
                    bx[here_rows, chunk(v + 2)] = res
                    acc[v // 16] = put(acc[v // 16], res, v, 61)
                epack[here_rows, pl.ds(0, LANES)] = acc[0]
                epack[here_rows, pl.ds(LANES, LANES)] = acc[1]

        loads[1].wait()
        widen(cy, cyb)
        for i in range(3):
            loads[4 + i].wait()
            x = sq[i]
            sq2[i, :, pl.ds(0, SIDE)] = x

        for i in range(3):
            x = sq2[i]
            sq2[i] = jnp.where(lanes_of((SIDE, LANES)) < SIDE, x, pltpu.roll(x, SIDE, 1))

        for i in range(3):
            @pl.loop(0, NV // 8)
            def _(k, i=i):
                for j in range(8):
                    v = k * 8 + j
                    row = jnp.where(low1, sq2[i, pl.ds(2 * v, 1), :], sq2[i, pl.ds(2 * v + 1, 1), :])
                    flat[i, :, chunk(v)] = jnp.broadcast_to(row, (8, LANES))

        loads[2].wait()
        loads[3].wait()
        diag = lax.broadcasted_iota(I32, (levels, levels), 0) == lax.broadcasted_iota(I32, (levels, levels), 1)
        for i, col in ((0, kcol), (1, pcol)):
            column = jnp.sum(jnp.where(diag, jnp.broadcast_to(kp[i], (levels, levels)), 0.0), axis=1, keepdims=True)
            col[...] = jnp.zeros((rows, LANES), F32)
            col[pl.ds(0, levels), :] = jnp.broadcast_to(column, (levels, LANES))
        inv = 1.0 / jnp.sum(kp[0], axis=1, keepdims=True)
        inv8 = jnp.broadcast_to(inv, (8, LANES))


        sset[pl.ds(0, packed), :] = squeeze(
            jnp.concatenate([roll(cy[:, chunk(1)], SIDE), cy[:, chunk(0)]], axis=1)
        )
        sset[pl.ds(packed + 4, 4), :] = jnp.zeros((4, LANES), F32)
        for i in range(2):
            for v in range(2):
                sset[pl.ds(packed + 2 * i + v, 1), :] = flat[1 + i, pl.ds(0, 1), chunk(v)]
        sets = []
        for d in range(2):
            copy = pltpu.make_async_remote_copy(
                src_ref=sset, dst_ref=rset.at[d], send_sem=sset_sem.at[d], recv_sem=rset_sem.at[d],
                device_id=(w, bwd(off_y[d])), device_id_type=MESH,
            )
            copy.start()
            sets.append(copy)

        x_interior()

        pack(cpack, cx, 0, 0)
        part = lanes_of((rows, 256)) & 3
        p1, p2, p3 = coefs(cpack[...])
        west1 = jnp.where(part == 0, p1, 0.0)
        west2 = jnp.where(part <= 1, p2, 0.0)
        west3 = jnp.where(part <= 2, p3, 0.0)
        cpack3 = (west1, west2, west3)

        def west_change(panel):
            panel = panel - ewrap[...]
            f = panel * cpack3[2] + roll2(panel, -1) * cpack3[1] + roll2(panel, -2) * cpack3[0]
            return jnp.where(part < 3, f - roll2(f, -1), 0.0)

        def y_flux(qv_r, q1, q1_r, q2_r, c):
            a1, a2, a3 = coefs(c)
            s1 = jnp.where(low, q1_r, qv_r)
            return s1 * a1 + q1 * a2 + jnp.where(low, q2_r, q1_r) * a3

        def y_interior(here_rows, finish, changed):
            none = jnp.zeros((8, LANES), F32)
            xs, rs, turned, outlet = {-1: none, -2: none}, {-1: none, -2: none}, {}, None
            done = {}
            lowest = 2 if changed else 0
            for v in range(NV):
                xs[v] = bx[here_rows, chunk(v + 2)]
                if changed:
                    change = dbuf[here_rows, pl.ds(v // 16 * LANES, LANES)]
                    xs[v] = xs[v] + jnp.where(l64_8 < 3, roll(change, -4 * (v % 16)), 0.0)
                    if v < 3:
                        bx[here_rows, chunk(v + 2)] = xs[v]
                rs[v] = roll(xs[v], SIDE)
                if v < lowest:
                    continue
                a1, a2, a3 = coefs(cy[here_rows, chunk(v)])
                flux = jnp.where(low8, rs[v - 1], rs[v]) * a1 + xs[v - 1] * a2 + jnp.where(low8, rs[v - 2], rs[v - 1]) * a3
                turned[v] = roll(flux, SIDE)
                done[v] = xs[v] + flux
                if v > lowest:
                    finish(v - 1, done[v - 1] - jnp.where(low8, turned[v - 1], turned[v]))
                if v == NV - 1:
                    outlet = xs[v] * a1 + jnp.where(low8, rs[v - 1], rs[v]) * a2 + xs[v - 1] * a3
                    finish(v, done[v] - jnp.where(low8, turned[v], outlet))

        def y_first(ta, pb):
            q0_, q1_, q2_ = bx[:, chunk(2)], bx[:, chunk(3)], bx[:, chunk(4)]
            t0, t1, t2 = roll(q0_, SIDE), roll(q1_, SIDE), roll(q2_, SIDE)
            tb = roll(pb, SIDE)
            above = roll(y_flux(t2, q1_, t1, t0, cy[:, chunk(2)]), SIDE)
            f1 = y_flux(t1, q0_, t0, tb, cy[:, chunk(1)])
            f0 = y_flux(t0, pb, tb, ta, cy[:, chunk(0)])
            g1, g0 = roll(f1, SIDE), roll(f0, SIDE)
            n1 = q1_ + f1 - jnp.where(low, g1, above) + emitted(1)
            n0 = q0_ + f0 - jnp.where(low, g0, g1) + emitted(0)
            return n0, n1

        def emitted(v):
            return pcol[...] * jnp.concatenate([flat[0, :, chunk(v)]] * (rows // 8), axis=0)

        def sum_levels(x):
            acc = x[0:8]
            for i in range(1, rows // 8):
                acc = acc + x[8 * i : 8 * i + 8]
            return acc

        def down(x):
            return jnp.broadcast_to(jnp.sum(x, axis=0, keepdims=True), (8, LANES))

        def tall(x):
            return jnp.concatenate([x] * (rows // 8), axis=0)

        before = permute(jnp.concatenate([epack[...], bx[:, pl.ds(CELLS, 256)]], axis=1), wy)
        panel = received(first, 0)
        dbuf[...] = west_change(panel)
        change = dbuf[:, pl.ds(LANES, LANES)]
        ends_now = [jnp.where(l64 < 3, roll(change, -4 * (v % 16)), 0.0) for v in (NV - 2, NV - 1)]
        res = before + permute(jnp.concatenate(ends_now, axis=1), wy, 256)
        for d in range(2):
            sy[d] = squeeze(res[:, d * 256 : (d + 1) * 256])
        y1 = []
        for d in range(2):
            copy = pltpu.make_async_remote_copy(
                src_ref=sy.at[d], dst_ref=ry.at[d], send_sem=s_sem.at[1, d], recv_sem=r_sem.at[1, d],
                device_id=(w, fwd(off_y[d])), device_id_type=MESH,
            )
            copy.start()
            y1.append(copy)
        pending.extend(y1)

        @pl.loop(0, tiles_of)
        def _(i):
            here_rows = tile_rows(i)
            acc = [jnp.zeros((8, LANES), F32)] * 2
            share = pcol[here_rows, :]

            def finish(v, res):
                res = res + share * flat[0, :, chunk(v)]
                q[here_rows, chunk(v)] = res
                acc[v // 16] = put(acc[v // 16], res, v, 61)

            y_interior(here_rows, finish, True)
            epack[here_rows, pl.ds(0, LANES)] = acc[0]
            epack[here_rows, pl.ds(LANES, LANES)] = acc[1]

        build(wyt, 3, off_y, 1, True)
        build(wxt, 0, off_x, 0, True)
        pack(cyp, cy, 0, 0)
        before = permute(jnp.concatenate([epack[...], q[:, pl.ds(CELLS - 256, 256)]], axis=1), wx)
        for copy in y1:
            copy.wait_recv()
        near_two, far_one = unsqueeze(ry[0] + ry[1])
        east = jnp.zeros((rows, LANES), F32)
        for v, res in enumerate(y_first(far_one, near_two)):
            q[:, chunk(v)] = res
            east = jnp.where(((l64 >> 2) == v) & ((l64 & 3) < 3), roll(res, 4 * v - 61), east)
        epack[:, pl.ds(0, LANES)] = epack[:, pl.ds(0, LANES)] + east
        strips = before + permute(east, wx)

        for d in range(2):
            sbuf[2, d] = tuck(strips[:, d * 256 : (d + 1) * 256])
        x2 = [send(2, d, fwd(off_x[d])) for d in range(2)]
        pending.extend(x2)
        x_interior()
        for copy in sets:
            copy.wait_recv()

        gf[...] = jnp.zeros((8, CELLS), F32)

        @pl.loop(0, tiles_of)
        def _(i):
            here_rows = tile_rows(i)
            share, weight = pcol[here_rows, :], kcol[here_rows, :]

            def finish(v, res):
                gf[:, chunk(v)] = gf[:, chunk(v)] + (res + share * flat[0, :, chunk(v)]) * weight

            y_interior(here_rows, finish, False)

        def slots(x):
            index = lanes_of(x.shape)
            return (index >> 6) & 1, (index >> 2) & 15

        def shift_down(x):
            high, u = slots(x[0])
            res = []
            for g in range(2):
                over = roll(x[g - 1], 4) if g > 0 else jnp.zeros_like(x[0])
                res.append(jnp.where(high == 1, roll(x[g], SIDE), jnp.where(u == 0, over, roll(x[g], 68))))
            return res

        def shift_down2(x):
            u = slots(x[0])[1]
            res = []
            for g in range(2):
                over = roll(x[g - 1], 68) if g > 0 else jnp.zeros_like(x[0])
                res.append(jnp.where(u == 0, over, roll(x[g], 4)))
            return res

        def shift_up(x, after):
            high, u = slots(x[0])
            res = []
            for g in range(2):
                over = roll(x[g + 1], 124) if g == 0 else after
                res.append(jnp.where(high == 0, roll(x[g], SIDE), jnp.where(u == 15, over, roll(x[g], 60))))
            return res

        ca = [coefs(cyp[:, pl.ds(g * LANES, LANES)]) for g in range(2)]
        k_all = kcol[...]
        zero = jnp.zeros((rows, LANES), F32)

        before = permute(jnp.concatenate([epack[...], bx[:, pl.ds(CELLS, 256)]], axis=1), wy)
        panel = received(x2, 2)
        dbuf[...] = west_change(panel)
        change = dbuf[:, pl.ds(LANES, LANES)]
        ends_now = [jnp.where(l64 < 3, roll(change, -4 * (v % 16)), 0.0) for v in (NV - 2, NV - 1)]
        panels = before + permute(jnp.concatenate(ends_now, axis=1), wy, 256)

        def misfit_weight(col, v_obs, v_pre):
            return v_pre * (col * inv8 - v_obs) * inv8

        new = [dbuf[:, pl.ds(g * LANES, LANES)] for g in range(2)]
        s1, s2 = shift_down(new), shift_down2(new)
        s3 = shift_down(s2)
        flow = [s1[g] * ca[g][0] + s2[g] * ca[g][1] + s3[g] * ca[g][2] for g in range(2)]
        out_flow = shift_up(flow, new[1] * ca[1][0] + s1[1] * ca[1][1] + s2[1] * ca[1][2])
        gained = [sum_levels((new[g] + flow[g] - out_flow[g]) * k_all) for g in range(2)]

        def column(v):
            return down(gf[:, chunk(v)] + jnp.where(l64_8 < 3, roll(gained[v // 16], -4 * (v % 16)), 0.0))

        for v in range(2):
            scol[:, chunk(v)] = column(v)[0:1]
        cols = []
        for d in range(2):
            copy = pltpu.make_async_remote_copy(
                src_ref=scol, dst_ref=rcol.at[d], send_sem=scol_sem.at[d], recv_sem=rcol_sem.at[d],
                device_id=(w, bwd(off_y[d])), device_id_type=MESH,
            )
            copy.start()
            cols.append(copy)

        effects, edge = [], []
        for d in range(2):
            pa, pb = panels[:, d * 256 : d * 256 + LANES], panels[:, d * 256 + LANES : d * 256 + 256]
            ra, rb = roll(pa, SIDE), roll(pb, SIDE)
            c0, c1 = unsqueeze(rset[d, pl.ds(0, packed), :])
            z1, z2, z3 = coefs(c0)
            o3 = coefs(c1)[2]
            edge.append((z1, z2, z3, o3))
            h0 = jnp.where(low, rb, 0.0) * z1 + pb * z2 + jnp.where(low, ra, rb) * z3
            h1 = jnp.where(low, rb, 0.0) * o3
            k0, k1 = roll(h0, SIDE), roll(h1, SIDE)
            d0 = h0 - jnp.where(low, k0, k1)
            d1 = h1 - jnp.where(low, k1, 0.0)
            effects.append((down(sum_levels(d0 * k_all)), down(sum_levels(d1 * k_all))))
            for v in range(2):
                sdc[d, :, chunk(v)] = effects[d][v][0:1]
        for d in range(2):
            copy = pltpu.make_async_remote_copy(
                src_ref=sdc.at[d], dst_ref=rdc.at[d], send_sem=s_sem.at[3, d], recv_sem=r_sem.at[3, d],
                device_id=(w, fwd(off_y[d])), device_id_type=MESH,
            )
            copy.start()
            pending.append(copy)

        def weigh(v, col):
            gf[:, chunk(v)] = misfit_weight(col, flat[1, :, chunk(v)], flat[2, :, chunk(v)])

        def slope(v):
            here = gf[:, chunk(v)]
            before = roll(gf[:, chunk(v - 1)], SIDE) if v > 0 else jnp.zeros((8, LANES), F32)
            return here - jnp.where(low8, before, roll(here, SIDE))

        for v in range(2, NV):
            weigh(v, column(v))
        gf[:, pl.ds(0, 256)] = jnp.zeros((8, 256), F32)
        for v in range(2, NV):
            df[:, chunk(v)] = slope(v)

        @pl.loop(0, tiles_of)
        def _(i):
            here_rows = tile_rows(i)
            weight = kcol[here_rows, :]
            none = jnp.zeros((8, LANES), F32)
            top = -weight * roll(gf[:, chunk(NV - 1)], SIDE)
            b1, b2, b3 = coefs(roll(cy[here_rows, chunk(NV - 1)], SIDE))
            first_up = roll(jnp.where(low8, top * b1, 0.0), SIDE)
            second_up = jnp.where(low8, top * b2, 0.0)
            third_up, third_up2 = roll(jnp.where(low8, top * b3, 0.0), SIDE), none
            acc = [none, none]
            for v in range(NV - 1, 1, -1):
                bar = weight * df[:, chunk(v)]
                a1, a2, a3 = coefs(cy[here_rows, chunk(v)])
                turned1, turned3 = roll(bar * a1, SIDE), roll(bar * a3, SIDE)
                res = (
                    weight * gf[:, chunk(v)]
                    + jnp.where(low8, turned1, first_up)
                    + second_up
                    + jnp.where(low8, third_up, third_up2)
                )
                mu[here_rows, chunk(v)] = res
                if v < NV - 2:
                    acc[v // 16] = put(acc[v // 16], res, v, 0)
                first_up, second_up, third_up, third_up2 = turned1, bar * a2, turned3, third_up
            dbuf[here_rows, pl.ds(0, LANES)] = acc[0]
            dbuf[here_rows, pl.ds(LANES, LANES)] = acc[1]

        bars = []
        for d in range(2):
            cols[d].wait_recv()
            z1, z2, z3, o3 = edge[d]
            w0, w1 = (
                misfit_weight(
                    jnp.broadcast_to(rcol[d, :, chunk(v)], (8, LANES)) + effects[d][v],
                    jnp.broadcast_to(rset[d, pl.ds(packed + v, 1), :], (8, LANES)),
                    jnp.broadcast_to(rset[d, pl.ds(packed + 2 + v, 1), :], (8, LANES)),
                )
                for v in range(2)
            )
            turned = roll(w0, SIDE)
            bar0 = k_all * tall(w0 - jnp.where(low8, 0.0, turned))
            bar1 = k_all * tall(w1 - jnp.where(low8, turned, roll(w1, SIDE)))
            third0, third1 = roll(bar0 * z3, SIDE), roll(bar1 * o3, SIDE)
            near_rows = jnp.where(low, 0.0, roll(bar0 * z1, SIDE)) + bar0 * z2 + jnp.where(low, third0, third1)
            far_rows = jnp.where(low, 0.0, third0)
            bars.append(jnp.concatenate([far_rows, near_rows], axis=1))
        back = permute(jnp.concatenate(bars, axis=1), wyt)
        back_east, back_north = back[:, :256], back[:, 256:]

        for copy in pending[-2:]:
            copy.wait_recv()
        for v in range(2):
            weigh(v, jnp.broadcast_to(scol[:, chunk(v)] + rdc[0, :, chunk(v)] + rdc[1, :, chunk(v)], (8, LANES)))
        made = {}
        for v in range(4):
            bar = k_all * tall(slope(v))
            a1, a2, a3 = coefs(cy[:, chunk(v)])
            made[v] = (roll(bar * a1, SIDE), bar * a2, roll(bar * a3, SIDE))
        for v in range(2):
            mu[:, chunk(v)] = (
                k_all * tall(gf[:, chunk(v)])
                + jnp.where(low, made[v][0], made[v + 1][0])
                + made[v + 1][1]
                + jnp.where(low, made[v + 1][2], made[v + 2][2])
            )
        mu[:, pl.ds(CELLS - 256, 256)] = mu[:, pl.ds(CELLS - 256, 256)] + back_north
        west0 = pack_group(mu, 0, 0, 0, range(2), dbuf[:, pl.ds(0, LANES)])
        west1_ = pack_group(mu, 1, 0, 0, range(14, 16), dbuf[:, pl.ds(LANES, LANES)])
        west = jnp.concatenate([west0, west1_], axis=1)
        diff = west - jnp.where(part > 0, roll2(west, 1), 0.0)
        pbar = diff * cpack3[2] + roll2(diff * cpack3[1], 1) + roll2(diff * cpack3[0], 2)
        p_all = pcol[...]
        for v in range(2):
            spb[:, chunk(v)] = down(sum_levels(pbar[:, v * LANES : (v + 1) * LANES] * p_all))[0:1]
        finals = []
        for r in range(windows):
            for d in range(2):
                copy = pltpu.make_async_remote_copy(
                    src_ref=spb, dst_ref=rpb.at[d, r], send_sem=spb_sem.at[d, r], recv_sem=rpb_sem.at[d, r],
                    device_id=(win_of(r), bwd(off_x[d])), device_id_type=MESH,
                )
                copy.start()
                finals.append(copy)

        bfix[...] = back_east
        both = jnp.broadcast_to(jnp.sum(kcol[...] * pcol[...], axis=0, keepdims=True), (8, LANES))
        sums = []
        for r in [*range(1, windows), 0]:
            to = win_of(r)
            side = lax.div(to * per, 16)
            east = bfix[:, chunk(side)]
            if per < 16:
                east = jnp.where(lax.rem(to * per, 16) == 8, roll(east, -32), east)
            for k in range(per):
                v = to * per + k
                whole = mu[:, chunk(v)] + jnp.where(l64 >= 61, roll(east, 61 - 4 * k), 0.0)
                m = whole * p_all
                c = cx[:, chunk(v)]
                a1, a2, a3 = coefs(jnp.where(l64 == 0, roll(c, 1), c))
                f = jnp.where(l64 == 0, 0.0, m) - roll(m, 1)
                s0 = sum_levels(m)
                s1, s2, s3 = sum_levels(f * a1), sum_levels(f * a2), sum_levels(f * a3)
                res = s0 + roll(s1, -1) + jnp.where(l64_8 < 63, roll(s2, -2), 0.0) + jnp.where(l64_8 < 62, roll(s3, -3), 0.0)
                gint[r, pl.ds(k, 1), :] = (down(res) + both * gf[:, chunk(v)])[0:1]
            if r > 0:
                copy = pltpu.make_async_remote_copy(
                    src_ref=gint.at[r], dst_ref=rg.at[r - 1],
                    send_sem=sg_sem.at[r - 1], recv_sem=rg_sem.at[r - 1],
                    device_id=(to, t), device_id_type=MESH,
                )
                copy.start()
                sums.append(copy)

        for copy in finals:
            copy.wait_recv()
        halves = []
        for d in range(2):
            acc = rpb[d, 0]
            for r in range(1, windows):
                acc = acc + rpb[d, r]
            halves.append(jnp.broadcast_to(acc, (8, 256)))
        ends = permute(jnp.concatenate(halves, axis=1), wxt)
        for v in range(NV):
            g, u = v // 16, v % 16
            row = jnp.where(l64_8 >= 61, roll(ends[:, g * LANES : (g + 1) * LANES], 61 - 4 * u), 0.0)
            if v >= NV - 2:
                at = 256 + (v - NV + 2) * LANES
                row = row + ends[:, at : at + LANES]
            fin[pl.ds(v, 1), :] = row[0:1]
        mine = pl.ds(pl.multiple_of(w * per, per), per)
        total = gint[0] + fin[mine, :]
        for copy in sums:
            copy.wait_recv()
        for r in range(1, windows):
            total = total + rg[r - 1]
        out[0, pl.ds(0, per, stride=2), :] = total[:, :SIDE]
        out[0, pl.ds(1, per, stride=2), :] = pltpu.roll(total, SIDE, 1)[:, :SIDE]

        for copy in pending + sets + cols + finals + sums:
            copy.wait_send()

    return kernel, rows, per


def body(initial, courant_x, courant_y, observed, precision_w, kernel, profile, emission, edges):
    levels = initial.shape[2]
    windows = lax.axis_size("win")
    run, rows, per = make_kernel(levels, windows)
    tiles_of = rows // 8
    packed = 8 * (tiles_of + tiles_of // 2 + (tiles_of % 2 == 1 and not 0 < levels % 8 <= 4))
    vm = pltpu.VMEM
    dma = pltpu.SemaphoreType.DMA
    anywhere = pl.BlockSpec(memory_space=pl.ANY)
    return pl.pallas_call(
        run,
        out_shape=pltpu.VMEM((1, 2 * per, SIDE), F32),
        in_specs=[anywhere] * 8 + [pl.BlockSpec(memory_space=pltpu.SMEM)],
        out_specs=pl.BlockSpec(memory_space=pltpu.VMEM),
        scratch_shapes=[
            vm((rows * NV, LANES), F32),
            vm((rows, CELLS), F32),
            vm((rows, CELLS + 256), F32),
            vm((rows, CELLS), F32),
            vm((rows, CELLS), F32),
            vm((rows, CELLS), F32),
            vm((levels, CELLS), BF16),
            vm((levels, CELLS), BF16),
            vm((3, SIDE, SIDE), F32),
            vm((3, SIDE, LANES), F32),
            vm((3, 8, CELLS), F32),
            vm((2, 1, levels), F32),
            vm((rows, LANES), F32),
            vm((rows, LANES), F32),
            vm((8, CELLS), F32),
            vm((8, CELLS), F32),
            vm((rows, 256), F32),
            vm((512, 512), BF16),
            vm((512, 512), BF16),
            vm((512, 512), BF16),
            vm((512, 512), BF16),
            vm((rows, 256), F32),
            vm((rows, 256), F32),
            vm((rows, 256), F32),
            vm((rows, 256), F32),
            vm((rows, 256), F32),
            vm((4, 2, rows - 8 * (tiles_of >= 4 and 0 < levels % 8 <= 4), 256), F32),
            vm((4, 2, rows - 8 * (tiles_of >= 4 and 0 < levels % 8 <= 4), 256), F32),
            vm((2, packed, LANES), F32),
            vm((2, packed, LANES), F32),
            vm((2, 1, 256), F32),
            vm((2, 1, 256), F32),
            vm((packed + 8, LANES), F32),
            vm((2, packed + 8, LANES), F32),
            vm((1, 256), F32),
            vm((2, 1, 256), F32),
            vm((1, 256), F32),
            vm((2, windows, 1, 256), F32),
            vm((windows, per, LANES), F32),
            vm((windows - 1, per, LANES), F32),
            vm((NV, LANES), F32),
            dma((7 + rows // 8,)),
            dma((4, 2)),
            dma((4, 2)),
            dma((2,)),
            dma((2,)),
            dma((2,)),
            dma((2,)),
            dma((2, windows)),
            dma((2, windows)),
            dma((windows - 1,)),
            dma((windows - 1,)),
        ],
        compiler_params=pltpu.CompilerParams(collective_id=0, has_side_effects=True),
    )(
        initial.reshape(levels * NV, LANES), courant_x, courant_y, observed, precision_w,
        kernel.reshape(1, levels), profile.reshape(1, levels), emission, edges,
    )


def solution(mesh):
    placed = (
        P("win", "tile", None, None),
        P("win", "tile", None, None),
        P("win", "tile", None, None),
        P("win", "tile", None, None),
        P("win", "tile", None, None),
        P(),
        P(),
        P("tile", None, None),
        P(),
    )
    return jax.shard_map(
        body, mesh=mesh, in_specs=placed, out_specs=P("tile", "win", None), check_vma=False
    )
```
